128 devices in a mesh: dp: 16 (over y, z), cls: 8 (over x, core).
Axes of the slice: x: 4, y: 4, z: 4, core: 2. Of those that a mesh axis runs over, the one named last changes fastest.
Arguments:
- particles: bfloat16 [16384, 2, 64, 128], P(('dp', 'cls')), may hold values from -128 to 128
- references: bfloat16 [200, 2, 64, 128], P('cls', None, 'dp'), may hold values from -6 to 6
- class_index: int32 [16384, 8], P(('dp', 'cls')), may hold values from 0 to 199, all different within a row
- rotation_index: int32 [16384, 8], P(('dp', 'cls')), may hold values from 0 to 35
- defocus_group: int32 [16384], P(('dp', 'cls')), may hold values from 0 to 127
- log_prior: float32 [16384, 8], P(('dp', 'cls')), may hold values from -3 to 400
- ctf_table: float32 [128, 64], replicated, may hold values from -1 to 1
Outputs:
- new_references: float32 [200, 2, 64, 128], P('cls', None, 'dp')
- responsibilities: float32 [16384, 8], P(('dp', 'cls'))
The draws below stay inside these ranges and needn't reach their ends.
Inputs may be any that keep to these rules, and one draw needn't show every extreme that they name: `class_index`: each row names 8 different classes; every class is named by some row.
All inputs are finite; a program needn't handle non-finite values.
Results may differ from the reference program's by a relative error of at most 0.0029.
Values may be sent and summed in bfloat16 or wider, within the bound.
No kernel may reach another device: no remote copies, remote signals or barrier semaphores. Data moves between devices by JAX's collectives and lax.ppermute only.
A program may use at most 128 MiB of HBM per device.

```python
import math
import jax
import jax.numpy as jnp
from jax import lax

CLASSES = 200
CYCLES = 64
HARM = 128
NROT = 36
TOPK = 8
GROUPS = 128
PARTICLES = 16384


def draw_log_prior(key, part):
    first = jax.random.fold_in(key, 0)
    values = jax.random.uniform(first, (PARTICLES, TOPK), jnp.float32, -3.0, 0.0)
    return values


def place_ends(values, own_key, low, largest):
    shape = values.shape
    spot = [jax.random.randint(jax.random.fold_in(own_key, axis), (), 0, shape[axis]) for axis in range(len(shape))]
    values = values.at[tuple(spot)].set(low)
    longest = shape.index(max(shape))
    spot[longest] = (spot[longest] + 1) % shape[longest]
    return values.at[tuple(spot)].set(largest)


def strengthened(drawn, rng, source, target, parts, factor):
    owner, partner = [(jnp.arange(drawn.shape[axis_at]) // (drawn.shape[axis_at] // parts)).reshape([-1 if axis == axis_at else 1 for axis in range(drawn.ndim)]) for axis_at in (source, target)]
    chosen = jax.random.permutation(rng, parts)[partner]
    strong = (owner == chosen) | (owner == (partner + parts // 2) % parts)
    return jnp.where(strong, factor * drawn, drawn)


def block_scale(rng, extent, cuts, smallest, largest):
    level = 1.0
    for position, shards_of in cuts:
        steps = jax.random.uniform(jax.random.fold_in(jax.random.fold_in(rng, 6), position), (shards_of,), jnp.float32, smallest / len(cuts), largest / len(cuts))
        level = level * jnp.repeat(jnp.exp(steps), extent[position] // shards_of).reshape((-1,) + (1,) * (len(extent) - 1 - position))
    return level


def choose_distinct(rng, rows, count, top, lift):
    order = jax.random.permutation(jax.random.fold_in(rng, 1), count)
    pull = order
    for power in range(3):
        pull = pull * pull // count
    pull = pull * lift // count
    chance = jax.random.randint(jax.random.fold_in(rng, 2), (rows, count), 0, 4096) + pull
    sure = jax.random.permutation(jax.random.fold_in(rng, 3), rows)[jnp.arange(count) % rows]
    chance = jnp.where(jnp.arange(rows)[:, None] == sure[None, :], 1 << 14, chance)
    score = chance * count + jnp.arange(count)
    return lax.top_k(score.astype(jnp.int32), top)[1].astype(jnp.int32)


def normal_values(stream_key, dims, width, reach, cuts=(), held_as=jnp.bfloat16):
    result = jax.random.normal(stream_key, dims, jnp.float32) * width
    if len(cuts) > 0:
        result = block_scale(stream_key, dims, cuts, -0.22, 0.18) * result
    return jnp.clip(result, min=-reach, max=reach).astype(held_as)


def gaussian_with(own_key, extent, width, bound, cuts, heavy, held_as=jnp.bfloat16):
    entries = width * jax.random.normal(own_key, extent, jnp.float32)
    if cuts:
        entries = entries * block_scale(own_key, extent, cuts, -0.22, 0.18)
    return jnp.clip(strengthened(entries, jax.random.fold_in(own_key, 3), *heavy), -bound, bound).astype(held_as)


def setup_inputs(seed: int = 0) -> dict:
    key_list = jax.random.split(jax.random.key(seed), 8)
    return {
        "particles": gaussian_with(key_list[0], (PARTICLES, 2, CYCLES, HARM), 8.0, 128.0, ((0, 128),), (0, 2, 64, 4.0)),
        "references": normal_values(key_list[1], (CLASSES, 2, CYCLES, HARM), 1.0, 6.0, ((0, 8), (2, 16))),
        "class_index": choose_distinct(key_list[2], PARTICLES, CLASSES, TOPK, 655),
        "rotation_index": place_ends(jax.random.randint(key_list[3], (PARTICLES, TOPK), 0, NROT), jax.random.fold_in(key_list[3], 1), 0, NROT - 1).astype(jnp.int32),
        "defocus_group": place_ends(jax.random.randint(key_list[4], (PARTICLES,), 0, GROUPS), jax.random.fold_in(key_list[4], 1), 0, GROUPS - 1).astype(jnp.int32),
        "log_prior": draw_log_prior(jax.random.fold_in(key_list[7], 71), 0),
        "ctf_table": jnp.clip(jax.random.uniform(key_list[6], (GROUPS, CYCLES), jnp.float32, -1.0, 1.0), -1.0, 1.0),
    }


SCORE_SCALE = 0.0025
REGULARIZER = 1.0


def phase_tables(rotations, harmonics):
    turns = (jnp.arange(rotations, dtype=jnp.int32)[:, None] * jnp.arange(harmonics, dtype=jnp.int32)[None, :]) % rotations
    angle = turns.astype(jnp.float32) * (2.0 * math.pi / rotations)
    return jnp.cos(angle), jnp.sin(angle)


def weigh_pairs(images, ctf_rows, cosine, sine, ref_rows, prior):
    scale = ctf_rows[:, None, :, None]
    real_part = images[:, None, 0, :, :].astype(jnp.float32)
    imag_part = images[:, None, 1, :, :].astype(jnp.float32)
    cos_rows = cosine[:, :, None, :]
    sin_rows = sine[:, :, None, :]
    rot_real = scale * (real_part * cos_rows - imag_part * sin_rows)
    rot_imag = scale * (real_part * sin_rows + imag_part * cos_rows)
    intersection = jnp.sum(rot_real * ref_rows[:, :, 0].astype(jnp.float32) + rot_imag * ref_rows[:, :, 1].astype(jnp.float32), axis=(2, 3))
    weights = jax.nn.softmax(prior + SCORE_SCALE * intersection, axis=-1)
    contribution = jnp.stack([weights[:, :, None, None] * rot_real, weights[:, :, None, None] * rot_imag], axis=2).astype(jnp.bfloat16)
    return weights, contribution


def reference(particles, references, class_index, rotation_index, defocus_group, log_prior, ctf_table):
    cosine_table, sine_table = phase_tables(NROT, HARM)
    per_block = min(PARTICLES, 256)
    num_blocks = PARTICLES // per_block

    def one_block(running, inputs):
        images, class_blk, rot_blk, group_blk, prior_blk = inputs
        ctf_rows = ctf_table[group_blk]
        ref_rows = references[class_blk]
        weights, contribution = weigh_pairs(images, ctf_rows, cosine_table[rot_blk], sine_table[rot_blk], ref_rows, prior_blk)
        flat_class = class_blk.reshape(-1)
        class_sums = running[0] + jax.ops.segment_sum(contribution.reshape(per_block * TOPK, 2 * CYCLES * HARM).astype(jnp.float32), flat_class, num_segments=CLASSES)
        squared = weights[:, :, None] * (ctf_rows * ctf_rows)[:, None, :]
        class_weight = running[1] + jax.ops.segment_sum(squared.reshape(per_block * TOPK, CYCLES), flat_class, num_segments=CLASSES)
        return (class_sums, class_weight), weights

    start = (jnp.zeros((CLASSES, 2 * CYCLES * HARM), jnp.float32), jnp.zeros((CLASSES, CYCLES), jnp.float32))
    inputs = (particles.reshape(num_blocks, per_block, 2, CYCLES, HARM),
              class_index.reshape(num_blocks, per_block, TOPK),
              rotation_index.reshape(num_blocks, per_block, TOPK),
              defocus_group.reshape(num_blocks, per_block),
              log_prior.reshape(num_blocks, per_block, TOPK))
    (class_sums, class_weight), weights = lax.scan(one_block, start, inputs)
    new_references = class_sums.reshape(CLASSES, 2, CYCLES, HARM) / (class_weight[:, None, :, None] + REGULARIZER)
    return new_references, weights.reshape(PARTICLES, TOPK)
```

```python
import math

import jax
import jax.numpy as jnp
import numpy as np
from jax import lax
from jax.experimental import pallas as pl
from jax.experimental.pallas import tpu as pltpu
from jax.sharding import PartitionSpec as P

NROT = 36
SCORE_SCALE = 0.0025
REGULARIZER = 1.0

F32 = jnp.float32
BF16 = jnp.bfloat16
LANES = 128
INDEX_ROWS = 32
VMEM_LIMIT = 56 * 1024 * 1024


def split3_np(x):
    hi = x.astype(jnp.bfloat16)
    rest = x - hi.astype(np.float32)
    mid = rest.astype(jnp.bfloat16)
    low = (rest - mid.astype(np.float32)).astype(jnp.bfloat16)
    return hi, mid, low


def rounded(x):
    return lax.reduce_precision(x, exponent_bits=8, mantissa_bits=7)


def split3(x):
    hi = rounded(x)
    rest = x - hi
    mid = rounded(rest)
    low = rounded(rest - mid)
    return hi.astype(BF16), mid.astype(BF16), low.astype(BF16)


def phase_table(harmonics):
    turns = (np.arange(NROT)[:, None] * np.arange(harmonics)[None, :]) % NROT
    angle = turns.astype(np.float32) * np.float32(2.0 * math.pi / NROT)
    both = np.concatenate([np.cos(angle), np.sin(angle)], axis=1).astype(np.float32)
    stacked = np.concatenate(split3_np(both), axis=0)
    pad = np.zeros((128 - 3 * NROT, 2 * harmonics), stacked.dtype)
    return np.concatenate([stacked, pad], axis=0)


def cut_kernel(share, x_ref, index_ref, out_ref, wide):
    step = pl.program_id(0)
    block, parts, cycles, lanes = x_ref.shape
    owners = out_ref.shape[0]
    total = block * pl.num_programs(0)
    rows = parts * cycles
    wide[...] = x_ref[...].astype(F32).reshape(block * rows, lanes)
    for owner in range(owners):
        for part in range(parts):
            for i in range(share):
                row = part * cycles + owner * share + i
                piece = wide[pl.ds(row, block, stride=rows), :]
                slab = part * share + i
                out_ref[owner, pl.ds(pl.multiple_of(slab * 128 + step * block, block), block), :] = piece.astype(BF16)

    @pl.when(step == 0)
    def _():
        for owner in range(owners):
            out_ref[owner, 2 * share * 128 :, :] = index_ref[...]


def cut_particles(particles, index_rows, owners):
    count, parts, cycles, lanes = particles.shape
    share = cycles // owners
    block = 32
    out_rows = 2 * share * count + INDEX_ROWS
    return pl.pallas_call(
        lambda *refs: cut_kernel(share, *refs),
        name="cut",
        grid=(count // block,),
        in_specs=[
            pl.BlockSpec((block, parts, cycles, lanes), lambda s: (s, 0, 0, 0)),
            pl.BlockSpec((INDEX_ROWS, lanes), lambda s: (0, 0)),
        ],
        out_specs=pl.BlockSpec((owners, out_rows, lanes), lambda s: (0, 0, 0)),
        out_shape=jax.ShapeDtypeStruct((owners, out_rows, lanes), BF16),
        scratch_shapes=[pltpu.VMEM((block * parts * cycles, lanes), F32)],
        compiler_params=pltpu.CompilerParams(vmem_limit_bytes=VMEM_LIMIT),
    )(particles, index_rows)


def lane_iota(rows, width):
    return lax.broadcasted_iota(jnp.int32, (rows, width), 1)


def transposed_index(rows):
    wide = jnp.concatenate([rows.astype(F32), jnp.zeros((LANES - INDEX_ROWS, LANES), F32)], axis=0)
    return wide.T


def scaled_particles(x_ref, columns, ctf_table, scaled, slabs):
    group = columns[:, 16:17]
    lanes = lane_iota(LANES, 384)
    hot = jnp.where(group == (lanes % 128).astype(F32), 1.0, 0.0).astype(BF16)
    ctf = jnp.dot(hot, ctf_table[...], preferred_element_type=F32)
    half = slabs // 2
    for slab in range(slabs):
        r = slab % half
        scaled[slab] = x_ref[0, slab * 128 : (slab + 1) * 128, :].astype(F32) * ctf[:, r * 128 : (r + 1) * 128]
    return hot


def rotation(columns, j, phases):
    lanes = lane_iota(LANES, 128)
    within = jnp.where(lanes < 3 * NROT, lanes % NROT, -1).astype(F32)
    hot = jnp.where(columns[:, 8 + j : 9 + j] == within, 1.0, 0.0).astype(BF16)
    both = jnp.dot(hot, phases[...], preferred_element_type=F32)
    return both[:, :128], both[:, 128:]


def score_kernel(slabs, top, x_ref, refs_ref, ctf_table, phases, out_ref, table, scaled):
    half = slabs // 2

    @pl.when(pl.program_id(0) == 0)
    def _():
        for dev in range(refs_ref.shape[0]):
            for slab in range(slabs):
                table[dev * 32 : (dev + 1) * 32, slab * 128 : (slab + 1) * 128] = refs_ref[dev, slab]

    columns = transposed_index(x_ref[0, slabs * 128 :, :])
    scaled_particles(x_ref, columns, ctf_table, scaled, slabs)
    classes = lane_iota(LANES, 256).astype(F32)
    lanes = lane_iota(LANES, LANES)
    scores = jnp.zeros((LANES, LANES), F32)
    for j in range(top):
        hot = jnp.where(columns[:, j : j + 1] == classes, 1.0, 0.0).astype(BF16)
        picked = jnp.dot(hot, table[...], preferred_element_type=F32)
        cosine, sine = rotation(columns, j, phases)
        even = odd = None
        for r in range(half):
            ref_re = picked[:, r * 128 : (r + 1) * 128]
            ref_im = picked[:, (half + r) * 128 : (half + r + 1) * 128]
            re, im = scaled[r], scaled[half + r]
            a = re * ref_re + im * ref_im
            b = re * ref_im - im * ref_re
            even = a if even is None else even + a
            odd = b if odd is None else odd + b
        total = jnp.sum(cosine * even + sine * odd, axis=1, keepdims=True)
        scores = jnp.where(lanes == j, total, scores)
    out_ref[0] = (SCORE_SCALE * scores).T[:top]


def partial_scores(moved, refs, ctf_table, phases, slabs, top):
    sources, rows, lanes = moved.shape
    whole = lambda a: pl.BlockSpec(a.shape, lambda s, n=a.ndim: (0,) * n)
    return pl.pallas_call(
        lambda *args: score_kernel(slabs, top, *args),
        name="score",
        grid=(sources,),
        in_specs=[pl.BlockSpec((1, rows, lanes), lambda s: (s, 0, 0)), whole(refs), whole(ctf_table), whole(phases)],
        out_specs=pl.BlockSpec((1, top, lanes), lambda s: (s, 0, 0)),
        out_shape=jax.ShapeDtypeStruct((sources, top, lanes), F32),
        scratch_shapes=[pltpu.VMEM((256, slabs * 128), BF16), pltpu.VMEM((slabs, 128, lanes), F32)],
        compiler_params=pltpu.CompilerParams(vmem_limit_bytes=VMEM_LIMIT),
    )(moved, refs, ctf_table, phases)


def sum_kernel(slabs, top, x_ref, partial_ref, ctf_table, ctf_lanes, phases, weight_ref, out_ref, scaled, contribution, hots, total, norm):
    half = slabs // 2
    step = pl.program_id(0)

    @pl.when(step == 0)
    def _():
        total[...] = jnp.zeros_like(total)
        norm[...] = jnp.zeros_like(norm)

    score = partial_ref[0, 0]
    for source in range(1, partial_ref.shape[0]):
        score = score + partial_ref[source, 0]
    raised = jnp.exp(score - jnp.max(score, axis=0, keepdims=True))
    weight = raised / jnp.sum(raised, axis=0, keepdims=True)
    weight_ref[0] = weight
    weight_columns = jnp.concatenate([weight, jnp.zeros((LANES - top, LANES), F32)], axis=0).T

    index_rows = x_ref[0, slabs * 128 :, :].astype(F32)
    columns = transposed_index(index_rows)
    group_hot = scaled_particles(x_ref, columns, ctf_table, scaled, slabs)
    classes = lax.broadcasted_iota(jnp.int32, (256, LANES), 0).astype(F32)
    spread = jnp.zeros((256, LANES), F32)
    for j in range(top):
        cosine, sine = rotation(columns, j, phases)
        w = weight_columns[:, j : j + 1]
        wc = w * cosine
        ws = w * sine
        for r in range(half):
            re, im = scaled[r], scaled[half + r]
            contribution[j * 128 : (j + 1) * 128, r * 128 : (r + 1) * 128] = (re * wc - im * ws).astype(BF16)
            contribution[j * 128 : (j + 1) * 128, (half + r) * 128 : (half + r + 1) * 128] = (re * ws + im * wc).astype(BF16)
        mine = index_rows[j : j + 1, :] == classes
        hots[:, j * 128 : (j + 1) * 128] = jnp.where(mine, 1.0, 0.0).astype(BF16)
        spread = jnp.where(mine, weight[j : j + 1, :], spread)
    total[...] += jnp.dot(hots[...], contribution[...], preferred_element_type=F32)
    ctf = jnp.dot(group_hot, ctf_lanes[...], preferred_element_type=F32)
    norm[...] += jnp.dot(spread, ctf * ctf, preferred_element_type=F32, precision=lax.Precision.HIGHEST)

    @pl.when(step == pl.num_programs(0) - 1)
    def _():
        n = norm[...]
        hi = n.astype(BF16)
        rest = n - hi.astype(F32)
        mid = rest.astype(BF16)
        low = (rest - mid.astype(F32)).astype(BF16)
        coded = jnp.where(
            lane_iota(256, LANES) < half,
            hi.astype(F32),
            jnp.where(
                lane_iota(256, LANES) < 2 * half,
                pltpu.roll(mid.astype(F32), half, 1),
                pltpu.roll(low.astype(F32), 2 * half, 1),
            ),
        ).astype(BF16)
        for dev in range(out_ref.shape[0]):
            rows = slice(dev * 32, (dev + 1) * 32)
            for slab in range(slabs):
                out_ref[dev, slab] = total[rows, slab * 128 : (slab + 1) * 128].astype(BF16)
            out_ref[dev, slabs] = coded[rows]


def weighted_sums(moved, partials, ctf_table, ctf_lanes, phases, slabs, top, owners):
    sources, rows, lanes = moved.shape
    whole = lambda a: pl.BlockSpec(a.shape, lambda s, n=a.ndim: (0,) * n)
    return pl.pallas_call(
        lambda *args: sum_kernel(slabs, top, *args),
        name="sums",
        grid=(sources,),
        in_specs=[
            pl.BlockSpec((1, rows, lanes), lambda s: (s, 0, 0)),
            pl.BlockSpec((sources, 1, top, lanes), lambda s: (0, s, 0, 0)),
            whole(ctf_table),
            whole(ctf_lanes),
            whole(phases),
        ],
        out_specs=[
            pl.BlockSpec((1, top, lanes), lambda s: (s, 0, 0)),
            pl.BlockSpec((owners, slabs + 1, 32, lanes), lambda s: (0, 0, 0, 0)),
        ],
        out_shape=[
            jax.ShapeDtypeStruct((sources, top, lanes), F32),
            jax.ShapeDtypeStruct((owners, slabs + 1, 32, lanes), BF16),
        ],
        scratch_shapes=[
            pltpu.VMEM((slabs, 128, lanes), F32),
            pltpu.VMEM((top * 128, slabs * 128), BF16),
            pltpu.VMEM((256, top * 128), BF16),
            pltpu.VMEM((256, slabs * 128), F32),
            pltpu.VMEM((256, lanes), F32),
        ],
        compiler_params=pltpu.CompilerParams(vmem_limit_bytes=VMEM_LIMIT),
    )(moved, partials, ctf_table, ctf_lanes, phases)


def finish_kernel(slabs, owned, parts_ref, out_ref):
    half = slabs // 2

    def gathered(slab):
        value = parts_ref[0, slab].astype(F32)
        for source in range(1, parts_ref.shape[0]):
            value = value + parts_ref[source, slab].astype(F32)
        return value

    coded = gathered(slabs)
    norm = coded + pltpu.roll(coded, LANES - half, 1) + pltpu.roll(coded, LANES - 2 * half, 1) + REGULARIZER
    for r in range(half):
        scale = 1.0 / norm[:, r : r + 1]
        for part in range(2):
            out_ref[:, part, r, :] = (gathered(part * half + r) * scale)[:owned]


def finish(parts, owned, slabs):
    return pl.pallas_call(
        lambda *args: finish_kernel(slabs, owned, *args),
        name="finish",
        out_shape=jax.ShapeDtypeStruct((owned, 2, slabs // 2, LANES), F32),
        compiler_params=pltpu.CompilerParams(vmem_limit_bytes=VMEM_LIMIT),
    )(parts)


def body(particles, references, class_index, rotation_index, defocus_group, log_prior, ctf_table):
    count, _, cycles, harmonics = particles.shape
    owned, _, share, _ = references.shape
    top = class_index.shape[1]
    owners = cycles // share
    slabs = 2 * share
    me = lax.axis_index("dp")

    padded = class_index + (32 - owned) * (class_index // owned)
    index_rows = jnp.concatenate(
        [padded, rotation_index, defocus_group[:, None], jnp.zeros((count, INDEX_ROWS - 2 * top - 1), jnp.int32)], axis=1
    )
    index_rows = index_rows.T.astype(BF16)
    send = cut_particles(particles, index_rows, owners)
    moved = lax.all_to_all(send, "dp", 0, 0)

    own_refs = jnp.pad(references.transpose(1, 2, 0, 3).reshape(slabs, owned, harmonics), ((0, 0), (0, 32 - owned), (0, 0)))
    refs = lax.all_gather(own_refs, "cls", axis=0)

    ctf = lax.dynamic_slice(ctf_table, (0, me * share), (ctf_table.shape[0], share))
    ctf_parts = jnp.concatenate(split3(ctf), axis=0)
    ctf_wide = jnp.broadcast_to(ctf_parts[:, :, None], ctf_parts.shape + (LANES,)).reshape(-1, share * LANES)
    ctf_lanes = jnp.pad(ctf_parts, ((0, 0), (0, LANES - share)))
    phases = jnp.asarray(phase_table(harmonics))

    partial = partial_scores(moved, refs, ctf_wide, phases, slabs, top)
    mine = (jnp.arange(owners) == me)[:, None, None]
    partial = partial + jnp.where(mine, log_prior.T[None], 0.0)
    partials = lax.all_to_all(jnp.broadcast_to(partial[None], (owners,) + partial.shape), "dp", 0, 0)

    weights, sums = weighted_sums(moved, partials, ctf_wide, ctf_lanes, phases, slabs, top, refs.shape[0])
    parts = lax.all_to_all(sums, "cls", 0, 0)
    new_references = finish(parts, owned, slabs)
    own_weights = lax.dynamic_index_in_dim(weights, me, 0, keepdims=False).T
    return new_references, own_weights


def solution(mesh):
    in_specs = (
        P(("dp", "cls"), None, None, None),
        P("cls", None, "dp", None),
        P(("dp", "cls"), None),
        P(("dp", "cls"), None),
        P(("dp", "cls")),
        P(("dp", "cls"), None),
        P(),
    )
    out_specs = (P("cls", None, "dp", None), P(("dp", "cls"), None))
    return jax.shard_map(body, mesh=mesh, in_specs=in_specs, out_specs=out_specs, check_vma=False)
```

```python
import math

import jax
import jax.numpy as jnp
import numpy as np
from jax import lax
from jax.experimental import pallas as pl
from jax.experimental.pallas import tpu as pltpu
from jax.sharding import PartitionSpec as P

NROT = 36
SCORE_SCALE = 0.0025
REGULARIZER = 1.0

F32 = jnp.float32
BF16 = jnp.bfloat16
LANES = 128
INDEX_ROWS = 32
VMEM_LIMIT = 56 * 1024 * 1024


def split3_np(x):
    hi = x.astype(jnp.bfloat16)
    rest = x - hi.astype(np.float32)
    mid = rest.astype(jnp.bfloat16)
    low = (rest - mid.astype(np.float32)).astype(jnp.bfloat16)
    return hi, mid, low


def rounded(x):
    return lax.reduce_precision(x, exponent_bits=8, mantissa_bits=7)


def split3(x):
    hi = rounded(x)
    rest = x - hi
    mid = rounded(rest)
    low = rounded(rest - mid)
    return hi.astype(BF16), mid.astype(BF16), low.astype(BF16)


def phase_table(harmonics):
    turns = (np.arange(NROT)[:, None] * np.arange(harmonics)[None, :]) % NROT
    angle = turns.astype(np.float32) * np.float32(2.0 * math.pi / NROT)
    both = np.concatenate([np.cos(angle), np.sin(angle)], axis=1).astype(np.float32)
    stacked = np.concatenate(split3_np(both), axis=0)
    pad = np.zeros((128 - 3 * NROT, 2 * harmonics), stacked.dtype)
    return np.concatenate([stacked, pad], axis=0).T


def cut_kernel(share, x_ref, index_ref, out_ref):
    step = pl.program_id(0)
    block, parts, cycles, lanes = x_ref.shape
    owners = out_ref.shape[0]
    for part in range(parts):
        for first in range(0, cycles, 8):
            swapped = jnp.swapaxes(x_ref[:, part, first : first + 8, :], 0, 1)
            for i in range(8):
                owner, slab = (first + i) // share, part * share + (first + i) % share
                out_ref[owner, pl.ds(pl.multiple_of(slab * 128 + step * block, block), block), :] = swapped[i]

    @pl.when(step == 0)
    def _():
        for owner in range(owners):
            out_ref[owner, 2 * share * 128 :, :] = index_ref[...]


def cut_particles(particles, index_rows, owners):
    count, parts, cycles, lanes = particles.shape
    share = cycles // owners
    block = 32
    out_rows = 2 * share * count + INDEX_ROWS
    return pl.pallas_call(
        lambda *refs: cut_kernel(share, *refs),
        name="cut",
        grid=(count // block,),
        in_specs=[
            pl.BlockSpec((block, parts, cycles, lanes), lambda s: (s, 0, 0, 0)),
            pl.BlockSpec((INDEX_ROWS, lanes), lambda s: (0, 0)),
        ],
        out_specs=pl.BlockSpec((owners, out_rows, lanes), lambda s: (0, 0, 0)),
        out_shape=jax.ShapeDtypeStruct((owners, out_rows, lanes), BF16),
        compiler_params=pltpu.CompilerParams(vmem_limit_bytes=VMEM_LIMIT),
    )(particles, index_rows)


def row_iota(rows):
    return lax.broadcasted_iota(jnp.int32, (rows, LANES), 0)


def hot_rows(row, wanted):
    return jnp.where(row == wanted, 1.0, 0.0).astype(BF16)


def ctf_rows(index_rows, ctf_parts):
    groups = hot_rows(index_rows[16:17], row_iota(LANES).astype(F32))
    three = jnp.dot(ctf_parts[...], groups, preferred_element_type=F32)
    return three[0:8] + three[8:16] + three[16:24]


def rotations(index_rows, top, phases):
    rows = row_iota(LANES)
    within = jnp.where(rows < 3 * NROT, rows % NROT, -1).astype(F32)
    hot = jnp.concatenate([hot_rows(index_rows[8 + j : 9 + j], within) for j in range(top)], axis=1)
    return jnp.dot(phases[...], hot, preferred_element_type=F32)


def prepare(s, slot, slabs, top, x_ref, ctf_parts, phases, index, ctf, scaled, angles):
    index[slot][...] = x_ref[s, slabs * 128 :, :].astype(F32)
    rows = index[slot][...]
    ctf[slot][...] = ctf_rows(rows, ctf_parts)
    for slab in range(slabs):
        r = slab % (slabs // 2)
        scaled[slot][slab] = x_ref[s, slab * 128 : (slab + 1) * 128, :].T.astype(F32) * ctf[slot][r : r + 1, :]
    angles[slot][...] = rotations(rows, top, phases)


def prepared_scratch(slabs, top):
    return [
        [pltpu.VMEM((INDEX_ROWS, LANES), F32)] * 2,
        [pltpu.VMEM((8, LANES), F32)] * 2,
        [pltpu.VMEM((slabs, 128, LANES), F32)] * 2,
        [pltpu.VMEM((256, top * 128), F32)] * 2,
    ]


def score_kernel(slabs, top, x_ref, refs_ref, ctf_parts, phases, out_ref, table, picked, index, ctf, scaled, angles):
    half = slabs // 2

    @pl.when(pl.program_id(0) == 0)
    def _():
        for slab in range(slabs):
            for piece in range(2):
                devs = [refs_ref[piece * 4 + dev, slab] for dev in range(4)]
                table[slab * 128 : (slab + 1) * 128, piece * 128 : (piece + 1) * 128] = jnp.concatenate(devs, axis=0).T.astype(BF16)

    classes = row_iota(256).astype(F32)

    def gather(slot, pair):
        hot = jnp.concatenate([hot_rows(index[slot][j : j + 1, :], classes) for j in (2 * pair, 2 * pair + 1)], axis=1)
        picked[pair % 2][...] = jnp.dot(table[...], hot, preferred_element_type=F32)

    def consume(slot, pair, side):
        j = 2 * pair + side
        across = slice(j * 128, (j + 1) * 128)
        here = slice(side * 128, (side + 1) * 128)
        even = odd = None
        for r in range(half):
            ref_re = picked[pair % 2][r * 128 : (r + 1) * 128, here]
            ref_im = picked[pair % 2][(half + r) * 128 : (half + r + 1) * 128, here]
            re, im = scaled[slot][r], scaled[slot][half + r]
            a = re * ref_re + im * ref_im
            b = re * ref_im - im * ref_re
            even = a if even is None else even + a
            odd = b if odd is None else odd + b
        return jnp.sum(angles[slot][:128, across] * even + angles[slot][128:, across] * odd, axis=0, keepdims=True)

    for s in range(x_ref.shape[0]):
        slot = s % 2
        prepare(s, slot, slabs, top, x_ref, ctf_parts, phases, index, ctf, scaled, angles)
        scores = []
        for pair in range(top // 2):
            gather(slot, pair)
            scores += [consume(slot, pair, 0), consume(slot, pair, 1)]
        out_ref[s] = SCORE_SCALE * jnp.concatenate(scores, axis=0)


def partial_scores(moved, refs, ctf_parts, phases, slabs, top):
    sources, rows, lanes = moved.shape
    whole = lambda a: pl.BlockSpec(a.shape, lambda s, n=a.ndim: (0,) * n)
    return pl.pallas_call(
        lambda *args: score_kernel(slabs, top, *args),
        name="score",
        grid=(sources // 2,),
        in_specs=[pl.BlockSpec((2, rows, lanes), lambda s: (s, 0, 0)), whole(refs), whole(ctf_parts), whole(phases)],
        out_specs=pl.BlockSpec((2, top, lanes), lambda s: (s, 0, 0)),
        out_shape=jax.ShapeDtypeStruct((sources, top, lanes), F32),
        scratch_shapes=[pltpu.VMEM((slabs * 128, 256), BF16), [pltpu.VMEM((slabs * 128, 256), F32)] * 2]
        + prepared_scratch(slabs, top),
        compiler_params=pltpu.CompilerParams(vmem_limit_bytes=VMEM_LIMIT),
    )(moved, refs, ctf_parts, phases)


def parted(x):
    hi = x.astype(BF16).astype(F32)
    rest = x - hi
    mid = rest.astype(BF16).astype(F32)
    return jnp.concatenate([hi, mid, rest - mid, jnp.zeros_like(x)], axis=0)


def sum_kernel(
    slabs, top, x_ref, partial_ref, ctf_parts, phases, weight_ref, out_ref, contribution, hots, total, index, ctf, scaled, angles
):
    half = slabs // 2
    sources = x_ref.shape[0]
    score = partial_ref[0]
    for source in range(1, sources):
        score = score + partial_ref[source]
    raised = jnp.exp(score - jnp.max(score, axis=1, keepdims=True))
    weight_ref[...] = raised / jnp.sum(raised, axis=1, keepdims=True)
    total[...] = jnp.zeros_like(total)
    contribution[1][...] = jnp.zeros_like(contribution[1][...])
    hots[1][...] = jnp.zeros_like(hots[1][...])
    classes = row_iota(256).astype(F32)

    def contribute(s, slot, j):
        across = slice(j * 128, (j + 1) * 128)
        w = weight_ref[s, j : j + 1, :]
        wc = w * angles[slot][:128, across]
        ws = w * angles[slot][128:, across]
        for r in range(half):
            re, im = scaled[slot][r], scaled[slot][half + r]
            contribution[slot][r * 128 : (r + 1) * 128, across] = (re * wc - im * ws).astype(BF16)
            contribution[slot][(half + r) * 128 : (half + r + 1) * 128, across] = (re * ws + im * wc).astype(BF16)
        contribution[slot][slabs * 128 :, across] = parted(w * (ctf[slot][...] * ctf[slot][...])).astype(BF16)
        hots[slot][:, across] = hot_rows(index[slot][j : j + 1, :], classes)

    def accumulate(slot):
        total[...] += lax.dot_general(
            contribution[slot][...], hots[slot][...], (((1,), (1,)), ((), ())), preferred_element_type=F32
        )

    def advance(s, slot):
        prepare(s, slot, slabs, top, x_ref, ctf_parts, phases, index, ctf, scaled, angles)
        accumulate(1 - slot)
        for j in range(top):
            contribute(s, slot, j)

    @pl.loop(0, sources // 2)
    def _(i):
        advance(2 * i, 0)
        advance(2 * i + 1, 1)

    accumulate(1)
    n = total[slabs * 128 :, :]
    coded = parted(n[0:8] + n[8:16] + n[16:24])
    coded = jnp.concatenate([coded, jnp.zeros((LANES - INDEX_ROWS, 256), F32)], axis=0)
    for slab in range(slabs + 1):
        piece = (total[slab * 128 : (slab + 1) * 128, :] if slab < slabs else coded).T.astype(BF16)
        for dev in range(out_ref.shape[0]):
            out_ref[dev, slab] = piece[dev * 32 : (dev + 1) * 32]


def weighted_sums(moved, partials, ctf_parts, phases, slabs, top, owners):
    sources, rows, lanes = moved.shape
    return pl.pallas_call(
        lambda *args: sum_kernel(slabs, top, *args),
        name="sums",
        out_shape=[
            jax.ShapeDtypeStruct((sources, top, lanes), F32),
            jax.ShapeDtypeStruct((owners, slabs + 1, 32, lanes), BF16),
        ],
        scratch_shapes=[
            [pltpu.VMEM((rows, top * 128), BF16)] * 2,
            [pltpu.VMEM((256, top * 128), BF16)] * 2,
            pltpu.VMEM((rows, 256), F32),
        ]
        + prepared_scratch(slabs, top),
        compiler_params=pltpu.CompilerParams(vmem_limit_bytes=VMEM_LIMIT),
    )(moved, partials, ctf_parts, phases)


def finish_kernel(slabs, owned, parts_ref, out_ref):
    half = slabs // 2

    def gathered(slab):
        value = parts_ref[0, slab].astype(F32)
        for source in range(1, parts_ref.shape[0]):
            value = value + parts_ref[source, slab].astype(F32)
        return value

    coded = gathered(slabs)
    norm = coded + pltpu.roll(coded, LANES - 8, 1) + pltpu.roll(coded, LANES - 16, 1) + REGULARIZER
    for r in range(half):
        scale = 1.0 / norm[:, r : r + 1]
        for part in range(2):
            out_ref[:, part, r, :] = (gathered(part * half + r) * scale)[:owned]


def finish(parts, owned, slabs):
    return pl.pallas_call(
        lambda *args: finish_kernel(slabs, owned, *args),
        name="finish",
        out_shape=jax.ShapeDtypeStruct((owned, 2, slabs // 2, LANES), F32),
        compiler_params=pltpu.CompilerParams(vmem_limit_bytes=VMEM_LIMIT),
    )(parts)


def body(particles, references, class_index, rotation_index, defocus_group, log_prior, ctf_table):
    count, _, cycles, harmonics = particles.shape
    owned, _, share, _ = references.shape
    top = class_index.shape[1]
    owners = cycles // share
    slabs = 2 * share
    me = lax.axis_index("dp")

    padded = class_index + (32 - owned) * (class_index // owned)
    index_rows = jnp.concatenate(
        [padded, rotation_index, defocus_group[:, None], jnp.zeros((count, INDEX_ROWS - 2 * top - 1), jnp.int32)], axis=1
    )
    index_rows = index_rows.T.astype(BF16)
    send = cut_particles(particles, index_rows, owners)
    moved = lax.all_to_all(send, "dp", 0, 0)

    own_refs = jnp.pad(references.transpose(1, 2, 0, 3).reshape(slabs, owned, harmonics), ((0, 0), (0, 32 - owned), (0, 0)))
    refs = lax.all_gather(own_refs.astype(F32), "cls", axis=0)

    ctf = lax.dynamic_slice(ctf_table, (0, me * share), (ctf_table.shape[0], share)).T
    ctf = jnp.pad(ctf, ((0, 8 - share), (0, 0)))
    ctf_parts = jnp.concatenate(split3(ctf), axis=0)
    phases = jnp.asarray(phase_table(harmonics))

    partial = partial_scores(moved, refs, ctf_parts, phases, slabs, top)
    mine = (jnp.arange(owners) == me)[:, None, None]
    partial = partial + jnp.where(mine, log_prior.T[None], 0.0)
    partials = lax.all_to_all(jnp.broadcast_to(partial[None], (owners,) + partial.shape), "dp", 0, 0)

    weights, sums = weighted_sums(moved, partials, ctf_parts, phases, slabs, top, refs.shape[0])
    parts = lax.all_to_all(sums, "cls", 0, 0)
    new_references = finish(parts, owned, slabs)
    own_weights = lax.dynamic_index_in_dim(weights, me, 0, keepdims=False).T
    return new_references, own_weights


def solution(mesh):
    in_specs = (
        P(("dp", "cls"), None, None, None),
        P("cls", None, "dp", None),
        P(("dp", "cls"), None),
        P(("dp", "cls"), None),
        P(("dp", "cls")),
        P(("dp", "cls"), None),
        P(),
    )
    out_specs = (P("cls", None, "dp", None), P(("dp", "cls"), None))
    return jax.shard_map(body, mesh=mesh, in_specs=in_specs, out_specs=out_specs, check_vma=False)
```

```python
import math

import jax
import jax.numpy as jnp
import numpy as np
from jax import lax
from jax.experimental import pallas as pl
from jax.experimental.pallas import tpu as pltpu
from jax.sharding import PartitionSpec as P

NROT = 36
SCORE_SCALE = 0.0025
REGULARIZER = 1.0

F32 = jnp.float32
BF16 = jnp.bfloat16
LANES = 128
INDEX_ROWS = 32
VMEM_LIMIT = 56 * 1024 * 1024


def split3_np(x):
    hi = x.astype(jnp.bfloat16)
    rest = x - hi.astype(np.float32)
    mid = rest.astype(jnp.bfloat16)
    low = (rest - mid.astype(np.float32)).astype(jnp.bfloat16)
    return hi, mid, low


def rounded(x):
    return lax.reduce_precision(x, exponent_bits=8, mantissa_bits=7)


def split3(x):
    hi = rounded(x)
    rest = x - hi
    mid = rounded(rest)
    low = rounded(rest - mid)
    return hi.astype(BF16), mid.astype(BF16), low.astype(BF16)


def phase_table(harmonics):
    turns = (np.arange(NROT)[:, None] * np.arange(harmonics)[None, :]) % NROT
    angle = turns.astype(np.float32) * np.float32(2.0 * math.pi / NROT)
    both = np.concatenate([np.cos(angle), np.sin(angle)], axis=1).astype(np.float32)
    stacked = np.concatenate(split3_np(both), axis=0)
    pad = np.zeros((128 - 3 * NROT, 2 * harmonics), stacked.dtype)
    return np.concatenate([stacked, pad], axis=0).T


def cut_kernel(share, x_ref, index_ref, out_ref):
    step = pl.program_id(0)
    block, parts, cycles, lanes = x_ref.shape
    owners = out_ref.shape[0]
    for part in range(parts):
        for first in range(0, cycles, 8):
            swapped = jnp.swapaxes(x_ref[:, part, first : first + 8, :], 0, 1)
            for i in range(8):
                owner, slab = (first + i) // share, part * share + (first + i) % share
                out_ref[owner, pl.ds(pl.multiple_of(slab * 128 + step * block, block), block), :] = swapped[i]

    @pl.when(step == 0)
    def _():
        for owner in range(owners):
            out_ref[owner, 2 * share * 128 :, :] = index_ref[...]


def cut_particles(particles, index_rows, owners):
    count, parts, cycles, lanes = particles.shape
    share = cycles // owners
    block = 32
    out_rows = 2 * share * count + INDEX_ROWS
    return pl.pallas_call(
        lambda *refs: cut_kernel(share, *refs),
        name="cut",
        grid=(count // block,),
        in_specs=[
            pl.BlockSpec((block, parts, cycles, lanes), lambda s: (s, 0, 0, 0)),
            pl.BlockSpec((INDEX_ROWS, lanes), lambda s: (0, 0)),
        ],
        out_specs=pl.BlockSpec((owners, out_rows, lanes), lambda s: (0, 0, 0)),
        out_shape=jax.ShapeDtypeStruct((owners, out_rows, lanes), BF16),
        compiler_params=pltpu.CompilerParams(vmem_limit_bytes=VMEM_LIMIT),
    )(particles, index_rows)


def row_iota(rows):
    return lax.broadcasted_iota(jnp.int32, (rows, LANES), 0)


def hot_rows(row, wanted):
    return jnp.where(row == wanted, 1.0, 0.0).astype(BF16)


def ctf_rows(index_rows, ctf_parts):
    groups = hot_rows(index_rows[16:17], row_iota(LANES).astype(F32))
    three = jnp.dot(ctf_parts[...], groups, preferred_element_type=F32)
    return three[0:8] + three[8:16] + three[16:24]


def rotations(index_rows, top, phases):
    rows = row_iota(LANES)
    within = jnp.where(rows < 3 * NROT, rows % NROT, -1).astype(F32)
    hot = jnp.concatenate([hot_rows(index_rows[8 + j : 9 + j], within) for j in range(top)], axis=1)
    return jnp.dot(phases[...], hot, preferred_element_type=F32)


def prepared(s, slabs, top, x_ref, ctf_parts, phases):
    rows = x_ref[s, slabs * 128 :, :].astype(F32)
    ctf = ctf_rows(rows, ctf_parts)
    scaled = []
    for slab in range(slabs):
        r = slab % (slabs // 2)
        scaled.append(x_ref[s, slab * 128 : (slab + 1) * 128, :].T.astype(F32) * ctf[r : r + 1, :])
    return rows, ctf, scaled, rotations(rows, top, phases)


def score_kernel(slabs, top, x_ref, refs_ref, ctf_parts, phases, prior_ref, out_ref, table):
    half = slabs // 2

    @pl.when(pl.program_id(0) == 0)
    def _():
        for slab in range(slabs):
            for piece in range(2):
                devs = [refs_ref[piece * 4 + dev, slab].astype(F32) for dev in range(4)]
                table[slab * 128 : (slab + 1) * 128, piece * 128 : (piece + 1) * 128] = jnp.concatenate(devs, axis=0).T.astype(BF16)

    classes = row_iota(256).astype(F32)

    for s in range(x_ref.shape[0]):
        index, _, scaled, angles = prepared(s, slabs, top, x_ref, ctf_parts, phases)
        scores = []
        for pair in range(top // 2):
            hot = jnp.concatenate([hot_rows(index[j : j + 1, :], classes) for j in (2 * pair, 2 * pair + 1)], axis=1)
            picked = jnp.dot(table[...], hot, preferred_element_type=F32)
            for side in range(2):
                across = slice((2 * pair + side) * 128, (2 * pair + side + 1) * 128)
                here = slice(side * 128, (side + 1) * 128)
                even = odd = None
                for r in range(half):
                    ref_re = picked[r * 128 : (r + 1) * 128, here]
                    ref_im = picked[(half + r) * 128 : (half + r + 1) * 128, here]
                    re, im = scaled[r], scaled[half + r]
                    a = re * ref_re + im * ref_im
                    b = re * ref_im - im * ref_re
                    even = a if even is None else even + a
                    odd = b if odd is None else odd + b
                scores.append(jnp.sum(angles[:128, across] * even + angles[128:, across] * odd, axis=0, keepdims=True))
        out_ref[s] = SCORE_SCALE * jnp.concatenate(scores, axis=0) + prior_ref[s]


def partial_scores(moved, refs, ctf_parts, phases, prior, slabs, top):
    sources, rows, lanes = moved.shape
    whole = lambda a: pl.BlockSpec(a.shape, lambda s, n=a.ndim: (0,) * n)
    return pl.pallas_call(
        lambda *args: score_kernel(slabs, top, *args),
        name="score",
        grid=(sources // 2,),
        in_specs=[
            pl.BlockSpec((2, rows, lanes), lambda s: (s, 0, 0)),
            whole(refs),
            whole(ctf_parts),
            whole(phases),
            pl.BlockSpec((2, top, lanes), lambda s: (s, 0, 0)),
        ],
        out_specs=pl.BlockSpec((2, top, lanes), lambda s: (s, 0, 0)),
        out_shape=jax.ShapeDtypeStruct((sources, top, lanes), F32),
        scratch_shapes=[pltpu.VMEM((slabs * 128, 256), BF16)],
        compiler_params=pltpu.CompilerParams(vmem_limit_bytes=VMEM_LIMIT),
    )(moved, refs, ctf_parts, phases, prior)


def parted(x):
    hi = x.astype(BF16).astype(F32)
    rest = x - hi
    mid = rest.astype(BF16).astype(F32)
    return jnp.concatenate([hi, mid, rest - mid, jnp.zeros_like(x)], axis=0)


def sum_kernel(slabs, top, x_ref, partial_ref, ctf_parts, phases, weight_ref, out_ref, total):
    half = slabs // 2
    step = pl.program_id(0)

    @pl.when(step == 0)
    def _():
        total[...] = jnp.zeros_like(total)

    classes = row_iota(256).astype(F32)
    score = partial_ref[0]
    for source in range(1, partial_ref.shape[0]):
        score = score + partial_ref[source]
    raised = jnp.exp(score - jnp.max(score, axis=1, keepdims=True))
    weights = raised / jnp.sum(raised, axis=1, keepdims=True)
    parts, hots = [], []
    for s in range(x_ref.shape[0]):
        index, ctf, scaled, angles = prepared(s, slabs, top, x_ref, ctf_parts, phases)
        squared = ctf * ctf
        weight = weights[s]
        for pair in range(top // 2):
            for j in (2 * pair, 2 * pair + 1):
                across = slice(j * 128, (j + 1) * 128)
                w = weight[j : j + 1, :]
                wc = w * angles[:128, across]
                ws = w * angles[128:, across]
                column = [(scaled[r] * wc - scaled[half + r] * ws).astype(BF16) for r in range(half)]
                column += [(scaled[r] * ws + scaled[half + r] * wc).astype(BF16) for r in range(half)]
                column.append(parted(w * squared).astype(BF16))
                parts.append(jnp.concatenate(column, axis=0))
                hots.append(hot_rows(index[j : j + 1, :], classes))
    total[...] += lax.dot_general(
        jnp.concatenate(parts, axis=1), jnp.concatenate(hots, axis=1), (((1,), (1,)), ((), ())), preferred_element_type=F32
    )
    weight_ref[...] = weights

    @pl.when(step == pl.num_programs(0) - 1)
    def _():
        n = total[slabs * 128 :, :]
        coded = parted(n[0:8] + n[8:16] + n[16:24])
        coded = jnp.concatenate([coded, jnp.zeros((LANES - INDEX_ROWS, 256), F32)], axis=0)
        for slab in range(slabs + 1):
            piece = (total[slab * 128 : (slab + 1) * 128, :] if slab < slabs else coded).T.astype(BF16)
            for dev in range(out_ref.shape[0]):
                out_ref[dev, slab] = piece[dev * 32 : (dev + 1) * 32]


def weighted_sums(moved, partials, ctf_parts, phases, slabs, top, owners):
    sources, rows, lanes = moved.shape
    whole = lambda a: pl.BlockSpec(a.shape, lambda s, n=a.ndim: (0,) * n)
    out = (owners, slabs + 1, 32, lanes)
    return pl.pallas_call(
        lambda *args: sum_kernel(slabs, top, *args),
        name="sums",
        grid=(sources // 4,),
        in_specs=[
            pl.BlockSpec((4, rows, lanes), lambda s: (s, 0, 0)),
            pl.BlockSpec((sources, 4, top, lanes), lambda s: (0, s, 0, 0)),
            whole(ctf_parts),
            whole(phases),
        ],
        out_specs=[
            pl.BlockSpec((4, top, lanes), lambda s: (s, 0, 0)),
            pl.BlockSpec(out, lambda s: (0, 0, 0, 0)),
        ],
        out_shape=[jax.ShapeDtypeStruct((sources, top, lanes), F32), jax.ShapeDtypeStruct(out, BF16)],
        scratch_shapes=[pltpu.VMEM((rows, 256), F32)],
        compiler_params=pltpu.CompilerParams(vmem_limit_bytes=VMEM_LIMIT),
    )(moved, partials, ctf_parts, phases)


def finish_kernel(slabs, owned, parts_ref, out_ref):
    half = slabs // 2

    def gathered(slab):
        value = parts_ref[0, slab].astype(F32)
        for source in range(1, parts_ref.shape[0]):
            value = value + parts_ref[source, slab].astype(F32)
        return value

    coded = gathered(slabs)
    norm = coded + pltpu.roll(coded, LANES - 8, 1) + pltpu.roll(coded, LANES - 16, 1) + REGULARIZER
    for r in range(half):
        scale = 1.0 / norm[:, r : r + 1]
        for part in range(2):
            out_ref[:, part, r, :] = (gathered(part * half + r) * scale)[:owned]


def finish(parts, owned, slabs):
    return pl.pallas_call(
        lambda *args: finish_kernel(slabs, owned, *args),
        name="finish",
        out_shape=jax.ShapeDtypeStruct((owned, 2, slabs // 2, LANES), F32),
        compiler_params=pltpu.CompilerParams(vmem_limit_bytes=VMEM_LIMIT),
    )(parts)


def body(particles, references, class_index, rotation_index, defocus_group, log_prior, ctf_table):
    count, _, cycles, harmonics = particles.shape
    owned, _, share, _ = references.shape
    top = class_index.shape[1]
    owners = cycles // share
    slabs = 2 * share
    me = lax.axis_index("dp")

    padded = class_index + (32 - owned) * (class_index // owned)
    index_rows = jnp.concatenate(
        [padded, rotation_index, defocus_group[:, None], jnp.zeros((count, INDEX_ROWS - 2 * top - 1), jnp.int32)], axis=1
    )
    index_rows = index_rows.T.astype(BF16)
    own_refs = jnp.pad(references.transpose(1, 2, 0, 3).reshape(slabs, owned, harmonics), ((0, 0), (0, 32 - owned), (0, 0)))
    refs = lax.all_gather(own_refs, "cls", axis=0)
    ctf = lax.dynamic_slice(ctf_table, (0, me * share), (ctf_table.shape[0], share)).T
    ctf = jnp.pad(ctf, ((0, 8 - share), (0, 0)))
    ctf_parts = jnp.concatenate(split3(ctf), axis=0)
    mine = (jnp.arange(owners) == me)[:, None, None]
    prior = jnp.where(mine, log_prior.T[None], 0.0)
    phases = jnp.asarray(phase_table(harmonics))

    send = cut_particles(particles, index_rows, owners)
    send, refs, ctf_parts, prior = lax.optimization_barrier((send, refs, ctf_parts, prior))
    moved = lax.all_to_all(send, "dp", 0, 0)
    partial = partial_scores(moved, refs, ctf_parts, phases, prior, slabs, top)
    partials = lax.all_to_all(jnp.broadcast_to(partial[None], (owners,) + partial.shape), "dp", 0, 0)

    weights, sums = weighted_sums(moved, partials, ctf_parts, phases, slabs, top, refs.shape[0])
    parts = lax.all_to_all(sums, "cls", 0, 0)
    new_references = finish(parts, owned, slabs)
    own_weights = lax.dynamic_index_in_dim(weights, me, 0, keepdims=False).T
    return new_references, own_weights


def solution(mesh):
    in_specs = (
        P(("dp", "cls"), None, None, None),
        P("cls", None, "dp", None),
        P(("dp", "cls"), None),
        P(("dp", "cls"), None),
        P(("dp", "cls")),
        P(("dp", "cls"), None),
        P(),
    )
    out_specs = (P("cls", None, "dp", None), P(("dp", "cls"), None))
    return jax.shard_map(body, mesh=mesh, in_specs=in_specs, out_specs=out_specs, check_vma=False)
```

```python
import math

import jax
import jax.numpy as jnp
import numpy as np
from jax import lax
from jax.experimental import pallas as pl
from jax.experimental.pallas import tpu as pltpu
from jax.sharding import PartitionSpec as P

NROT = 36
SCORE_SCALE = 0.0025
REGULARIZER = 1.0

F32 = jnp.float32
BF16 = jnp.bfloat16
LANES = 128
INDEX_ROWS = 32
VMEM_LIMIT = 56 * 1024 * 1024


def split3_np(x):
    hi = x.astype(jnp.bfloat16)
    rest = x - hi.astype(np.float32)
    mid = rest.astype(jnp.bfloat16)
    low = (rest - mid.astype(np.float32)).astype(jnp.bfloat16)
    return hi, mid, low


def rounded(x):
    return lax.reduce_precision(x, exponent_bits=8, mantissa_bits=7)


def split3(x):
    hi = rounded(x)
    rest = x - hi
    mid = rounded(rest)
    low = rounded(rest - mid)
    return hi.astype(BF16), mid.astype(BF16), low.astype(BF16)


def phase_table(harmonics):
    turns = (np.arange(NROT)[:, None] * np.arange(harmonics)[None, :]) % NROT
    angle = turns.astype(np.float32) * np.float32(2.0 * math.pi / NROT)
    both = np.concatenate([np.cos(angle), np.sin(angle)], axis=1).astype(np.float32)
    stacked = np.concatenate(split3_np(both), axis=0)
    pad = np.zeros((128 - 3 * NROT, 2 * harmonics), stacked.dtype)
    return np.concatenate([stacked, pad], axis=0).T


def cut_kernel(share, x_ref, index_ref, out_ref):
    step = pl.program_id(0)
    block, parts, cycles, lanes = x_ref.shape
    owners = out_ref.shape[0]
    for part in range(parts):
        for first in range(0, cycles, 8):
            swapped = jnp.swapaxes(x_ref[:, part, first : first + 8, :], 0, 1)
            for i in range(8):
                owner, slab = (first + i) // share, part * share + (first + i) % share
                out_ref[owner, pl.ds(pl.multiple_of(slab * 128 + step * block, block), block), :] = swapped[i]

    @pl.when(step == 0)
    def _():
        for owner in range(owners):
            out_ref[owner, 2 * share * 128 :, :] = index_ref[...]


def cut_particles(particles, index_rows, owners):
    count, parts, cycles, lanes = particles.shape
    share = cycles // owners
    block = 32
    out_rows = 2 * share * count + INDEX_ROWS
    return pl.pallas_call(
        lambda *refs: cut_kernel(share, *refs),
        name="cut",
        grid=(count // block,),
        in_specs=[
            pl.BlockSpec((block, parts, cycles, lanes), lambda s: (s, 0, 0, 0)),
            pl.BlockSpec((INDEX_ROWS, lanes), lambda s: (0, 0)),
        ],
        out_specs=pl.BlockSpec((owners, out_rows, lanes), lambda s: (0, 0, 0)),
        out_shape=jax.ShapeDtypeStruct((owners, out_rows, lanes), BF16),
        compiler_params=pltpu.CompilerParams(vmem_limit_bytes=VMEM_LIMIT),
    )(particles, index_rows)


def row_iota(rows):
    return lax.broadcasted_iota(jnp.int32, (rows, LANES), 0)


def hot_rows(row, wanted):
    return jnp.where(row == wanted, 1.0, 0.0).astype(BF16)


def ctf_rows(index_rows, ctf_parts):
    groups = hot_rows(index_rows[16:17], row_iota(LANES).astype(F32))
    three = jnp.dot(ctf_parts[...], groups, preferred_element_type=F32)
    return three[0:8] + three[8:16] + three[16:24]


def rotations(index_rows, top, phases):
    rows = row_iota(LANES)
    within = jnp.where(rows < 3 * NROT, rows % NROT, -1).astype(F32)
    hot = jnp.concatenate([hot_rows(index_rows[8 + j : 9 + j], within) for j in range(top)], axis=1)
    return jnp.dot(phases[...], hot, preferred_element_type=F32)


def prepared(s, slabs, top, x_ref, ctf_parts, phases):
    rows = x_ref[s, slabs * 128 :, :].astype(F32)
    ctf = ctf_rows(rows, ctf_parts)
    scaled = []
    for slab in range(slabs):
        r = slab % (slabs // 2)
        scaled.append(x_ref[s, slab * 128 : (slab + 1) * 128, :].T.astype(F32) * ctf[r : r + 1, :])
    return rows, ctf, scaled, rotations(rows, top, phases)


def score_kernel(slabs, top, x_ref, refs_ref, ctf_parts, phases, prior_ref, out_ref, table):
    half = slabs // 2

    @pl.when(pl.program_id(0) == 0)
    def _():
        for slab in range(slabs):
            for piece in range(2):
                devs = [refs_ref[piece * 4 + dev, slab] for dev in range(4)]
                table[slab * 128 : (slab + 1) * 128, piece * 128 : (piece + 1) * 128] = jnp.concatenate(devs, axis=0).T.astype(BF16)

    classes = row_iota(256).astype(F32)

    for s in range(x_ref.shape[0]):
        index, _, scaled, angles = prepared(s, slabs, top, x_ref, ctf_parts, phases)
        scores = []
        for pair in range(top // 2):
            hot = jnp.concatenate([hot_rows(index[j : j + 1, :], classes) for j in (2 * pair, 2 * pair + 1)], axis=1)
            evens, odds = [None, None], [None, None]
            for r in range(half):
                ref_re = jnp.dot(table[r * 128 : (r + 1) * 128, :], hot, preferred_element_type=F32)
                ref_im = jnp.dot(table[(half + r) * 128 : (half + r + 1) * 128, :], hot, preferred_element_type=F32)
                re, im = scaled[r], scaled[half + r]
                for side in range(2):
                    here = slice(side * 128, (side + 1) * 128)
                    a = re * ref_re[:, here] + im * ref_im[:, here]
                    b = re * ref_im[:, here] - im * ref_re[:, here]
                    evens[side] = a if r == 0 else evens[side] + a
                    odds[side] = b if r == 0 else odds[side] + b
            for side in range(2):
                across = slice((2 * pair + side) * 128, (2 * pair + side + 1) * 128)
                scores.append(jnp.sum(angles[:128, across] * evens[side] + angles[128:, across] * odds[side], axis=0, keepdims=True))
        score = SCORE_SCALE * jnp.concatenate(scores, axis=0) + prior_ref[s]
        for owner in range(out_ref.shape[0]):
            out_ref[owner, s] = score


def partial_scores(moved, refs, ctf_parts, phases, prior, slabs, top):
    sources, rows, lanes = moved.shape
    whole = lambda a: pl.BlockSpec(a.shape, lambda s, n=a.ndim: (0,) * n)
    return pl.pallas_call(
        lambda *args: score_kernel(slabs, top, *args),
        name="score",
        grid=(sources // 2,),
        in_specs=[
            pl.BlockSpec((2, rows, lanes), lambda s: (s, 0, 0)),
            whole(refs),
            whole(ctf_parts),
            whole(phases),
            pl.BlockSpec((2, top, lanes), lambda s: (s, 0, 0)),
        ],
        out_specs=pl.BlockSpec((sources, 2, top, lanes), lambda s: (0, s, 0, 0)),
        out_shape=jax.ShapeDtypeStruct((sources, sources, top, lanes), F32),
        scratch_shapes=[pltpu.VMEM((slabs * 128, 256), BF16)],
        compiler_params=pltpu.CompilerParams(vmem_limit_bytes=VMEM_LIMIT),
    )(moved, refs, ctf_parts, phases, prior)


def parted(x):
    hi = x.astype(BF16).astype(F32)
    rest = x - hi
    mid = rest.astype(BF16).astype(F32)
    return jnp.concatenate([hi, mid, rest - mid, jnp.zeros_like(x)], axis=0)


def sum_kernel(slabs, top, x_ref, partial_ref, ctf_parts, phases, weight_ref, out_ref, total):
    half = slabs // 2
    step = pl.program_id(0)

    @pl.when(step == 0)
    def _():
        total[...] = jnp.zeros_like(total)

    classes = row_iota(256).astype(F32)
    score = partial_ref[0]
    for source in range(1, partial_ref.shape[0]):
        score = score + partial_ref[source]
    raised = jnp.exp(score - jnp.max(score, axis=1, keepdims=True))
    weights = raised / jnp.sum(raised, axis=1, keepdims=True)
    parts, hots = [], []
    for s in range(x_ref.shape[0]):
        index, ctf, scaled, angles = prepared(s, slabs, top, x_ref, ctf_parts, phases)
        squared = ctf * ctf
        weight = weights[s]
        for pair in range(top // 2):
            for j in (2 * pair, 2 * pair + 1):
                across = slice(j * 128, (j + 1) * 128)
                w = weight[j : j + 1, :]
                wc = w * angles[:128, across]
                ws = w * angles[128:, across]
                column = [(scaled[r] * wc - scaled[half + r] * ws).astype(BF16) for r in range(half)]
                column += [(scaled[r] * ws + scaled[half + r] * wc).astype(BF16) for r in range(half)]
                column.append(parted(w * squared).astype(BF16))
                parts.append(jnp.concatenate(column, axis=0))
                hots.append(hot_rows(index[j : j + 1, :], classes))
    total[...] += lax.dot_general(
        jnp.concatenate(parts, axis=1), jnp.concatenate(hots, axis=1), (((1,), (1,)), ((), ())), preferred_element_type=F32
    )
    weight_ref[...] = weights

    @pl.when(step == pl.num_programs(0) - 1)
    def _():
        n = total[slabs * 128 :, :]
        coded = parted(n[0:8] + n[8:16] + n[16:24])
        coded = jnp.concatenate([coded, jnp.zeros((LANES - INDEX_ROWS, 256), F32)], axis=0)
        for slab in range(slabs + 1):
            piece = (total[slab * 128 : (slab + 1) * 128, :] if slab < slabs else coded).T.astype(BF16)
            for dev in range(out_ref.shape[0]):
                out_ref[dev, slab] = piece[dev * 32 : (dev + 1) * 32]


def weighted_sums(moved, partials, ctf_parts, phases, slabs, top, owners):
    sources, rows, lanes = moved.shape
    whole = lambda a: pl.BlockSpec(a.shape, lambda s, n=a.ndim: (0,) * n)
    out = (owners, slabs + 1, 32, lanes)
    return pl.pallas_call(
        lambda *args: sum_kernel(slabs, top, *args),
        name="sums",
        grid=(sources // 4,),
        in_specs=[
            pl.BlockSpec((4, rows, lanes), lambda s: (s, 0, 0)),
            pl.BlockSpec((sources, 4, top, lanes), lambda s: (0, s, 0, 0)),
            whole(ctf_parts),
            whole(phases),
        ],
        out_specs=[
            pl.BlockSpec((4, top, lanes), lambda s: (s, 0, 0)),
            pl.BlockSpec(out, lambda s: (0, 0, 0, 0)),
        ],
        out_shape=[jax.ShapeDtypeStruct((sources, top, lanes), F32), jax.ShapeDtypeStruct(out, BF16)],
        scratch_shapes=[pltpu.VMEM((rows, 256), F32)],
        compiler_params=pltpu.CompilerParams(vmem_limit_bytes=VMEM_LIMIT),
    )(moved, partials, ctf_parts, phases)


def finish_kernel(slabs, owned, parts_ref, out_ref):
    half = slabs // 2

    def gathered(slab):
        value = parts_ref[0, slab].astype(F32)
        for source in range(1, parts_ref.shape[0]):
            value = value + parts_ref[source, slab].astype(F32)
        return value

    coded = gathered(slabs)
    norm = coded + pltpu.roll(coded, LANES - 8, 1) + pltpu.roll(coded, LANES - 16, 1) + REGULARIZER
    for r in range(half):
        scale = 1.0 / norm[:, r : r + 1]
        for part in range(2):
            out_ref[:, part, r, :] = (gathered(part * half + r) * scale)[:owned]


def finish(parts, owned, slabs):
    return pl.pallas_call(
        lambda *args: finish_kernel(slabs, owned, *args),
        name="finish",
        out_shape=jax.ShapeDtypeStruct((owned, 2, slabs // 2, LANES), F32),
        compiler_params=pltpu.CompilerParams(vmem_limit_bytes=VMEM_LIMIT),
    )(parts)


def body(particles, references, class_index, rotation_index, defocus_group, log_prior, ctf_table):
    count, _, cycles, harmonics = particles.shape
    owned, _, share, _ = references.shape
    top = class_index.shape[1]
    owners = cycles // share
    slabs = 2 * share
    me = lax.axis_index("dp")

    padded = class_index + (32 - owned) * (class_index // owned)
    index_rows = jnp.concatenate(
        [padded, rotation_index, defocus_group[:, None], jnp.zeros((count, INDEX_ROWS - 2 * top - 1), jnp.int32)], axis=1
    )
    index_rows = index_rows.T.astype(BF16)
    own_refs = jnp.pad(references.transpose(1, 2, 0, 3).reshape(slabs, owned, harmonics), ((0, 0), (0, 32 - owned), (0, 0)))
    refs = lax.all_gather(own_refs.astype(F32), "cls", axis=0)
    ctf = lax.dynamic_slice(ctf_table, (0, me * share), (ctf_table.shape[0], share)).T
    ctf = jnp.pad(ctf, ((0, 8 - share), (0, 0)))
    ctf_parts = jnp.concatenate(split3(ctf), axis=0)
    mine = (jnp.arange(owners) == me)[:, None, None]
    prior = jnp.where(mine, log_prior.T[None], 0.0)
    phases = jnp.asarray(phase_table(harmonics))

    send = cut_particles(particles, index_rows, owners)
    moved = lax.cond(defocus_group[0] >= 0, lambda a: lax.all_to_all(a, "dp", 0, 0), lambda a: a, send)
    partial = partial_scores(moved, refs, ctf_parts, phases, prior, slabs, top)
    partials = lax.all_to_all(partial, "dp", 0, 0)

    weights, sums = weighted_sums(moved, partials, ctf_parts, phases, slabs, top, refs.shape[0])
    parts = lax.all_to_all(sums, "cls", 0, 0)
    new_references = finish(parts, owned, slabs)
    own_weights = lax.dynamic_index_in_dim(weights, me, 0, keepdims=False).T
    return new_references, own_weights


def solution(mesh):
    in_specs = (
        P(("dp", "cls"), None, None, None),
        P("cls", None, "dp", None),
        P(("dp", "cls"), None),
        P(("dp", "cls"), None),
        P(("dp", "cls")),
        P(("dp", "cls"), None),
        P(),
    )
    out_specs = (P("cls", None, "dp", None), P(("dp", "cls"), None))
    return jax.shard_map(body, mesh=mesh, in_specs=in_specs, out_specs=out_specs, check_vma=False)
```

```python
import math

import jax
import jax.numpy as jnp
import numpy as np
from jax import lax
from jax.experimental import pallas as pl
from jax.experimental.pallas import tpu as pltpu
from jax.sharding import PartitionSpec as P

NROT = 36
SCORE_SCALE = 0.0025
REGULARIZER = 1.0

F32 = jnp.float32
BF16 = jnp.bfloat16
LANES = 128
INDEX_ROWS = 32
VMEM_LIMIT = 56 * 1024 * 1024


def split3_np(x):
    hi = x.astype(jnp.bfloat16)
    rest = x - hi.astype(np.float32)
    mid = rest.astype(jnp.bfloat16)
    low = (rest - mid.astype(np.float32)).astype(jnp.bfloat16)
    return hi, mid, low


def rounded(x):
    return lax.reduce_precision(x, exponent_bits=8, mantissa_bits=7)


def split3(x):
    hi = rounded(x)
    rest = x - hi
    mid = rounded(rest)
    low = rounded(rest - mid)
    return hi.astype(BF16), mid.astype(BF16), low.astype(BF16)


def phase_table(harmonics):
    turns = (np.arange(NROT)[:, None] * np.arange(harmonics)[None, :]) % NROT
    angle = turns.astype(np.float32) * np.float32(2.0 * math.pi / NROT)
    both = np.concatenate([np.cos(angle), np.sin(angle)], axis=1).astype(np.float32)
    stacked = np.concatenate(split3_np(both), axis=0)
    pad = np.zeros((128 - 3 * NROT, 2 * harmonics), stacked.dtype)
    return np.concatenate([stacked, pad], axis=0).T


def cut_kernel(share, owned, x_ref, class_ref, rotation_ref, group_ref, out_ref):
    step = pl.program_id(0)
    block, parts, cycles, lanes = x_ref.shape
    owners = out_ref.shape[0]
    for part in range(parts):
        for first in range(0, cycles, 8):
            swapped = jnp.swapaxes(x_ref[:, part, first : first + 8, :], 0, 1)
            for i in range(8):
                owner, slab = (first + i) // share, part * share + (first + i) % share
                out_ref[owner, pl.ds(pl.multiple_of(slab * 128 + step * block, block), block), :] = swapped[i]

    @pl.when(step == 0)
    def _():
        padded = class_ref[...]
        for k in range(1, 256 // 32):
            padded = padded + jnp.where(class_ref[...] >= k * owned, 32 - owned, 0)
        group = jnp.broadcast_to(group_ref[...], padded.shape)
        rows = jnp.concatenate([padded, rotation_ref[...], group, jnp.zeros_like(padded)], axis=0)
        rows = rows.astype(F32).astype(BF16)
        for owner in range(owners):
            out_ref[owner, 2 * share * 128 :, :] = rows


def cut_particles(particles, classes, rotations, groups, owners, owned):
    count, parts, cycles, lanes = particles.shape
    share = cycles // owners
    block = 32
    out_rows = 2 * share * count + INDEX_ROWS
    index = [pl.BlockSpec(a.shape, lambda s: (0, 0)) for a in (classes, rotations, groups)]
    return pl.pallas_call(
        lambda *refs: cut_kernel(share, owned, *refs),
        name="cut",
        grid=(count // block,),
        in_specs=[pl.BlockSpec((block, parts, cycles, lanes), lambda s: (s, 0, 0, 0))] + index,
        out_specs=pl.BlockSpec((owners, out_rows, lanes), lambda s: (0, 0, 0)),
        out_shape=jax.ShapeDtypeStruct((owners, out_rows, lanes), BF16),
        cost_estimate=pl.CostEstimate(flops=0, bytes_accessed=4 * particles.size, transcendentals=0),
        compiler_params=pltpu.CompilerParams(vmem_limit_bytes=VMEM_LIMIT),
    )(particles, classes, rotations, groups)


def row_iota(rows):
    return lax.broadcasted_iota(jnp.int32, (rows, LANES), 0)


def hot_rows(row, wanted):
    return jnp.where(row == wanted, 1.0, 0.0).astype(BF16)


def ctf_rows(index_rows, ctf_parts):
    groups = hot_rows(index_rows[16:17], row_iota(LANES).astype(F32))
    three = jnp.dot(ctf_parts[...], groups, preferred_element_type=F32)
    return three[0:8] + three[8:16] + three[16:24]


def rotations(index_rows, top, phases):
    rows = row_iota(LANES)
    within = jnp.where(rows < 3 * NROT, rows % NROT, -1).astype(F32)
    hot = jnp.concatenate([hot_rows(index_rows[8 + j : 9 + j], within) for j in range(top)], axis=1)
    return jnp.dot(phases[...], hot, preferred_element_type=F32)


def prepared(s, slabs, top, x_ref, ctf_parts, phases):
    rows = x_ref[s, slabs * 128 :, :].astype(F32)
    ctf = ctf_rows(rows, ctf_parts)
    scaled = []
    for slab in range(slabs):
        r = slab % (slabs // 2)
        scaled.append(x_ref[s, slab * 128 : (slab + 1) * 128, :].T.astype(F32) * ctf[r : r + 1, :])
    return rows, ctf, scaled, rotations(rows, top, phases)


def score_kernel(slabs, top, x_ref, refs_ref, ctf_parts, phases, prior_ref, me_ref, out_ref, table):
    half = slabs // 2

    @pl.when(pl.program_id(0) == 0)
    def _():
        for slab in range(slabs):
            for piece in range(2):
                devs = [refs_ref[piece * 4 + dev, slab].astype(F32) for dev in range(4)]
                table[slab * 128 : (slab + 1) * 128, piece * 128 : (piece + 1) * 128] = jnp.concatenate(devs, axis=0).T.astype(BF16)

    classes = row_iota(256).astype(F32)

    for s in range(x_ref.shape[0]):
        index, _, scaled, angles = prepared(s, slabs, top, x_ref, ctf_parts, phases)
        scores = []
        for pair in range(top // 2):
            hot = jnp.concatenate([hot_rows(index[j : j + 1, :], classes) for j in (2 * pair, 2 * pair + 1)], axis=1)
            evens, odds = [None, None], [None, None]
            for r in range(half):
                ref_re = jnp.dot(table[r * 128 : (r + 1) * 128, :], hot, preferred_element_type=F32)
                ref_im = jnp.dot(table[(half + r) * 128 : (half + r + 1) * 128, :], hot, preferred_element_type=F32)
                re, im = scaled[r], scaled[half + r]
                for side in range(2):
                    here = slice(side * 128, (side + 1) * 128)
                    a = re * ref_re[:, here] + im * ref_im[:, here]
                    b = re * ref_im[:, here] - im * ref_re[:, here]
                    evens[side] = a if r == 0 else evens[side] + a
                    odds[side] = b if r == 0 else odds[side] + b
            for side in range(2):
                across = slice((2 * pair + side) * 128, (2 * pair + side + 1) * 128)
                scores.append(jnp.sum(angles[:128, across] * evens[side] + angles[128:, across] * odds[side], axis=0, keepdims=True))
        own = pl.program_id(0) * x_ref.shape[0] + s == me_ref[0]
        score = SCORE_SCALE * jnp.concatenate(scores, axis=0) + jnp.where(own, prior_ref[...], 0.0)
        for owner in range(out_ref.shape[0]):
            out_ref[owner, s] = score


def partial_scores(moved, refs, ctf_parts, phases, prior, me, slabs, top):
    sources, rows, lanes = moved.shape
    whole = lambda a: pl.BlockSpec(a.shape, lambda s, n=a.ndim: (0,) * n)
    return pl.pallas_call(
        lambda *args: score_kernel(slabs, top, *args),
        name="score",
        grid=(sources // 2,),
        in_specs=[
            pl.BlockSpec((2, rows, lanes), lambda s: (s, 0, 0)),
            whole(refs),
            whole(ctf_parts),
            whole(phases),
            whole(prior),
            pl.BlockSpec(memory_space=pltpu.SMEM),
        ],
        out_specs=pl.BlockSpec((sources, 2, top, lanes), lambda s: (0, s, 0, 0)),
        out_shape=jax.ShapeDtypeStruct((sources, sources, top, lanes), F32),
        scratch_shapes=[pltpu.VMEM((slabs * 128, 256), BF16)],
        compiler_params=pltpu.CompilerParams(vmem_limit_bytes=VMEM_LIMIT),
    )(moved, refs, ctf_parts, phases, prior, me.astype(jnp.int32).reshape(1))


def parted(x):
    hi = x.astype(BF16).astype(F32)
    rest = x - hi
    mid = rest.astype(BF16).astype(F32)
    return jnp.concatenate([hi, mid, rest - mid, jnp.zeros_like(x)], axis=0)


def sum_kernel(slabs, top, x_ref, partial_ref, ctf_parts, phases, weight_ref, out_ref, total):
    half = slabs // 2
    step = pl.program_id(0)

    @pl.when(step == 0)
    def _():
        total[...] = jnp.zeros_like(total)

    classes = row_iota(256).astype(F32)
    score = partial_ref[0]
    for source in range(1, partial_ref.shape[0]):
        score = score + partial_ref[source]
    raised = jnp.exp(score - jnp.max(score, axis=1, keepdims=True))
    weights = raised / jnp.sum(raised, axis=1, keepdims=True)
    parts, hots = [], []
    for s in range(x_ref.shape[0]):
        index, ctf, scaled, angles = prepared(s, slabs, top, x_ref, ctf_parts, phases)
        squared = ctf * ctf
        weight = weights[s]
        for pair in range(top // 2):
            for j in (2 * pair, 2 * pair + 1):
                across = slice(j * 128, (j + 1) * 128)
                w = weight[j : j + 1, :]
                wc = w * angles[:128, across]
                ws = w * angles[128:, across]
                column = [(scaled[r] * wc - scaled[half + r] * ws).astype(BF16) for r in range(half)]
                column += [(scaled[r] * ws + scaled[half + r] * wc).astype(BF16) for r in range(half)]
                column.append(parted(w * squared).astype(BF16))
                parts.append(jnp.concatenate(column, axis=0))
                hots.append(hot_rows(index[j : j + 1, :], classes))
    total[...] += lax.dot_general(
        jnp.concatenate(parts, axis=1), jnp.concatenate(hots, axis=1), (((1,), (1,)), ((), ())), preferred_element_type=F32
    )
    weight_ref[...] = weights

    @pl.when(step == pl.num_programs(0) - 1)
    def _():
        n = total[slabs * 128 :, :]
        coded = parted(n[0:8] + n[8:16] + n[16:24])
        coded = jnp.concatenate([coded, jnp.zeros((LANES - INDEX_ROWS, 256), F32)], axis=0)
        for slab in range(slabs + 1):
            piece = (total[slab * 128 : (slab + 1) * 128, :] if slab < slabs else coded).T.astype(BF16)
            for dev in range(out_ref.shape[0]):
                out_ref[dev, slab] = piece[dev * 32 : (dev + 1) * 32]


def weighted_sums(moved, partials, ctf_parts, phases, slabs, top, owners):
    sources, rows, lanes = moved.shape
    whole = lambda a: pl.BlockSpec(a.shape, lambda s, n=a.ndim: (0,) * n)
    out = (owners, slabs + 1, 32, lanes)
    return pl.pallas_call(
        lambda *args: sum_kernel(slabs, top, *args),
        name="sums",
        grid=(sources // 4,),
        in_specs=[
            pl.BlockSpec((4, rows, lanes), lambda s: (s, 0, 0)),
            pl.BlockSpec((sources, 4, top, lanes), lambda s: (0, s, 0, 0)),
            whole(ctf_parts),
            whole(phases),
        ],
        out_specs=[
            pl.BlockSpec((4, top, lanes), lambda s: (s, 0, 0)),
            pl.BlockSpec(out, lambda s: (0, 0, 0, 0)),
        ],
        out_shape=[jax.ShapeDtypeStruct((sources, top, lanes), F32), jax.ShapeDtypeStruct(out, BF16)],
        scratch_shapes=[pltpu.VMEM((rows, 256), F32)],
        compiler_params=pltpu.CompilerParams(vmem_limit_bytes=VMEM_LIMIT),
    )(moved, partials, ctf_parts, phases)


def finish_kernel(slabs, owned, parts_ref, out_ref):
    half = slabs // 2

    def gathered(slab):
        value = parts_ref[0, slab].astype(F32)
        for source in range(1, parts_ref.shape[0]):
            value = value + parts_ref[source, slab].astype(F32)
        return value

    coded = gathered(slabs)
    norm = coded + pltpu.roll(coded, LANES - 8, 1) + pltpu.roll(coded, LANES - 16, 1) + REGULARIZER
    for r in range(half):
        scale = 1.0 / norm[:, r : r + 1]
        for part in range(2):
            out_ref[:, part, r, :] = (gathered(part * half + r) * scale)[:owned]


def finish(parts, owned, slabs):
    return pl.pallas_call(
        lambda *args: finish_kernel(slabs, owned, *args),
        name="finish",
        out_shape=jax.ShapeDtypeStruct((owned, 2, slabs // 2, LANES), F32),
        compiler_params=pltpu.CompilerParams(vmem_limit_bytes=VMEM_LIMIT),
    )(parts)


def body(particles, references, class_index, rotation_index, defocus_group, log_prior, ctf_table):
    count, _, cycles, harmonics = particles.shape
    owned, _, share, _ = references.shape
    top = class_index.shape[1]
    owners = cycles // share
    slabs = 2 * share
    me = lax.axis_index("dp")

    own_refs = jnp.pad(references.transpose(1, 2, 0, 3).reshape(slabs, owned, harmonics), ((0, 0), (0, 32 - owned), (0, 0)))
    holders = lax.axis_size("cls")
    refs = lax.all_to_all(jnp.broadcast_to(own_refs[None], (holders,) + own_refs.shape), "cls", 0, 0)
    ctf = lax.dynamic_slice(ctf_table, (0, me * share), (ctf_table.shape[0], share)).T
    ctf = jnp.pad(ctf, ((0, 8 - share), (0, 0)))
    ctf_parts = jnp.concatenate(split3(ctf), axis=0)
    phases = jnp.asarray(phase_table(harmonics))

    send = cut_particles(particles, class_index.T, rotation_index.T, defocus_group[None], owners, owned)
    send, refs, ctf_parts = lax.optimization_barrier((send, refs, ctf_parts))
    moved = lax.all_to_all(send, "dp", 0, 0)
    partial = partial_scores(moved, refs, ctf_parts, phases, log_prior.T, me, slabs, top)
    partials = lax.all_to_all(partial, "dp", 0, 0)

    weights, sums = weighted_sums(moved, partials, ctf_parts, phases, slabs, top, refs.shape[0])
    parts = lax.all_to_all(sums, "cls", 0, 0)
    new_references = finish(parts, owned, slabs)
    own_weights = lax.dynamic_index_in_dim(weights, me, 0, keepdims=False).T
    return new_references, own_weights


def solution(mesh):
    in_specs = (
        P(("dp", "cls"), None, None, None),
        P("cls", None, "dp", None),
        P(("dp", "cls"), None),
        P(("dp", "cls"), None),
        P(("dp", "cls")),
        P(("dp", "cls"), None),
        P(),
    )
    out_specs = (P("cls", None, "dp", None), P(("dp", "cls"), None))
    return jax.shard_map(body, mesh=mesh, in_specs=in_specs, out_specs=out_specs, check_vma=False)
```

```python
import math

import jax
import jax.numpy as jnp
import numpy as np
from jax import lax
from jax.experimental import pallas as pl
from jax.experimental.pallas import tpu as pltpu
from jax.sharding import PartitionSpec as P

NROT = 36
SCORE_SCALE = 0.0025
REGULARIZER = 1.0

F32 = jnp.float32
BF16 = jnp.bfloat16
LANES = 128
INDEX_ROWS = 32
VMEM_LIMIT = 56 * 1024 * 1024


def split3_np(x):
    hi = x.astype(jnp.bfloat16)
    rest = x - hi.astype(np.float32)
    mid = rest.astype(jnp.bfloat16)
    low = (rest - mid.astype(np.float32)).astype(jnp.bfloat16)
    return hi, mid, low


def rounded(x):
    return lax.reduce_precision(x, exponent_bits=8, mantissa_bits=7)


def split3(x):
    hi = rounded(x)
    rest = x - hi
    mid = rounded(rest)
    low = rounded(rest - mid)
    return hi.astype(BF16), mid.astype(BF16), low.astype(BF16)


def phase_table(harmonics):
    turns = (np.arange(NROT)[:, None] * np.arange(harmonics)[None, :]) % NROT
    angle = turns.astype(np.float32) * np.float32(2.0 * math.pi / NROT)
    both = np.concatenate([np.cos(angle), np.sin(angle)], axis=1).astype(np.float32)
    stacked = np.concatenate(split3_np(both), axis=0)
    pad = np.zeros((128 - 3 * NROT, 2 * harmonics), stacked.dtype)
    return np.concatenate([stacked, pad], axis=0).T


def cut_kernel(share, owned, x_ref, class_ref, rotation_ref, group_ref, out_ref):
    step = pl.program_id(0)
    block, parts, cycles, lanes = x_ref.shape
    owners = out_ref.shape[0]
    for part in range(parts):
        for first in range(0, cycles, 8):
            swapped = jnp.swapaxes(x_ref[:, part, first : first + 8, :], 0, 1)
            for i in range(8):
                owner, slab = (first + i) // share, part * share + (first + i) % share
                out_ref[owner, pl.ds(pl.multiple_of(slab * 128 + step * block, block), block), :] = swapped[i]

    @pl.when(step == 0)
    def _():
        padded = class_ref[...]
        for k in range(1, 256 // 32):
            padded = padded + jnp.where(class_ref[...] >= k * owned, 32 - owned, 0)
        group = jnp.broadcast_to(group_ref[...], padded.shape)
        rows = jnp.concatenate([padded, rotation_ref[...], group, jnp.zeros_like(padded)], axis=0)
        rows = rows.astype(F32).astype(BF16)
        for owner in range(owners):
            out_ref[owner, 2 * share * 128 :, :] = rows


def cut_particles(particles, classes, rotations, groups, owners, owned):
    count, parts, cycles, lanes = particles.shape
    share = cycles // owners
    block = 32
    out_rows = 2 * share * count + INDEX_ROWS
    index = [pl.BlockSpec(a.shape, lambda s: (0, 0)) for a in (classes, rotations, groups)]
    return pl.pallas_call(
        lambda *refs: cut_kernel(share, owned, *refs),
        name="cut",
        grid=(count // block,),
        in_specs=[pl.BlockSpec((block, parts, cycles, lanes), lambda s: (s, 0, 0, 0))] + index,
        out_specs=pl.BlockSpec((owners, out_rows, lanes), lambda s: (0, 0, 0)),
        out_shape=jax.ShapeDtypeStruct((owners, out_rows, lanes), BF16),
        cost_estimate=pl.CostEstimate(flops=0, bytes_accessed=4 * particles.size, transcendentals=0),
        compiler_params=pltpu.CompilerParams(vmem_limit_bytes=VMEM_LIMIT),
    )(particles, classes, rotations, groups)


def row_iota(rows):
    return lax.broadcasted_iota(jnp.int32, (rows, LANES), 0)


def hot_rows(row, wanted):
    return jnp.where(row.astype(BF16) == wanted.astype(BF16), BF16(1.0), BF16(0.0))


def ctf_rows(index_rows, ctf_parts):
    groups = hot_rows(index_rows[16:17], row_iota(LANES).astype(F32))
    three = jnp.dot(ctf_parts[...], groups, preferred_element_type=F32)
    return three[0:8] + three[8:16] + three[16:24]


def rotations(index_rows, top, phases):
    rows = row_iota(LANES)
    within = jnp.where(rows < 3 * NROT, rows % NROT, -1).astype(F32)
    hot = jnp.concatenate([hot_rows(index_rows[8 + j : 9 + j], within) for j in range(top)], axis=1)
    return jnp.dot(phases[...], hot, preferred_element_type=F32)


def prepared(s, slabs, top, x_ref, ctf_parts, phases):
    rows = x_ref[s, slabs * 128 :, :].astype(F32)
    ctf = ctf_rows(rows, ctf_parts)
    scaled = []
    for slab in range(slabs):
        r = slab % (slabs // 2)
        scaled.append(x_ref[s, slab * 128 : (slab + 1) * 128, :].T.astype(F32) * ctf[r : r + 1, :])
    return rows, ctf, scaled, rotations(rows, top, phases)


def score_kernel(slabs, top, x_ref, refs_ref, ctf_parts, phases, prior_ref, me_ref, out_ref, table, stage, padded):
    half = slabs // 2

    @pl.when(pl.program_id(0) == 0)
    def _():
        owned = stage.shape[0] // slabs
        padded[...] = jnp.zeros_like(padded)
        for dev in range(refs_ref.shape[0]):
            stage[...] = refs_ref[dev].astype(F32)
            for slab in range(slabs):
                padded[slab, dev * 32 : dev * 32 + owned, :] = stage[pl.ds(slab, owned, stride=slabs), :]
        for slab in range(slabs):
            rows = slice(slab * 128, (slab + 1) * 128)
            for piece in range(2):
                across = slice(piece * 128, (piece + 1) * 128)
                table[rows, across] = padded[slab, across, :].T.astype(BF16)

    classes = row_iota(256).astype(F32)

    for s in range(x_ref.shape[0]):
        index, _, scaled, angles = prepared(s, slabs, top, x_ref, ctf_parts, phases)
        scores = []
        for pair in range(top // 2):
            hot = jnp.concatenate([hot_rows(index[j : j + 1, :], classes) for j in (2 * pair, 2 * pair + 1)], axis=1)
            evens, odds = [None, None], [None, None]
            for r in range(half):
                ref_re = jnp.dot(table[r * 128 : (r + 1) * 128, :], hot, preferred_element_type=F32)
                ref_im = jnp.dot(table[(half + r) * 128 : (half + r + 1) * 128, :], hot, preferred_element_type=F32)
                re, im = scaled[r], scaled[half + r]
                for side in range(2):
                    here = slice(side * 128, (side + 1) * 128)
                    a = re * ref_re[:, here] + im * ref_im[:, here]
                    b = re * ref_im[:, here] - im * ref_re[:, here]
                    evens[side] = a if r == 0 else evens[side] + a
                    odds[side] = b if r == 0 else odds[side] + b
            for side in range(2):
                across = slice((2 * pair + side) * 128, (2 * pair + side + 1) * 128)
                scores.append(jnp.sum(angles[:128, across] * evens[side] + angles[128:, across] * odds[side], axis=0, keepdims=True))
        own = pl.program_id(0) * x_ref.shape[0] + s == me_ref[0]
        score = SCORE_SCALE * jnp.concatenate(scores, axis=0) + jnp.where(own, prior_ref[...], 0.0)
        for owner in range(out_ref.shape[0]):
            out_ref[owner, s] = score


def partial_scores(moved, refs, ctf_parts, phases, prior, me, slabs, top):
    sources, rows, lanes = moved.shape
    whole = lambda a: pl.BlockSpec(a.shape, lambda s, n=a.ndim: (0,) * n)
    return pl.pallas_call(
        lambda *args: score_kernel(slabs, top, *args),
        name="score",
        grid=(sources // 4,),
        in_specs=[
            pl.BlockSpec((4, rows, lanes), lambda s: (s, 0, 0)),
            whole(refs),
            whole(ctf_parts),
            whole(phases),
            whole(prior),
            pl.BlockSpec(memory_space=pltpu.SMEM),
        ],
        out_specs=pl.BlockSpec((sources, 4, top, lanes), lambda s: (0, s, 0, 0)),
        out_shape=jax.ShapeDtypeStruct((sources, sources, top, lanes), F32),
        scratch_shapes=[
            pltpu.VMEM((slabs * 128, 256), BF16),
            pltpu.VMEM(refs.shape[1:], F32),
            pltpu.VMEM((slabs, 256, lanes), F32),
        ],
        compiler_params=pltpu.CompilerParams(vmem_limit_bytes=VMEM_LIMIT),
    )(moved, refs, ctf_parts, phases, prior, me.astype(jnp.int32).reshape(1))


def parted(x):
    hi = x.astype(BF16).astype(F32)
    rest = x - hi
    mid = rest.astype(BF16).astype(F32)
    return jnp.concatenate([hi, mid, rest - mid, jnp.zeros_like(x)], axis=0)


def sum_kernel(slabs, top, x_ref, partial_ref, ctf_parts, phases, weight_ref, out_ref, total):
    half = slabs // 2
    step = pl.program_id(0)

    @pl.when(step == 0)
    def _():
        total[...] = jnp.zeros_like(total)

    classes = row_iota(256).astype(F32)
    score = partial_ref[0]
    for source in range(1, partial_ref.shape[0]):
        score = score + partial_ref[source]
    raised = jnp.exp(score - jnp.max(score, axis=1, keepdims=True))
    weights = raised / jnp.sum(raised, axis=1, keepdims=True)
    parts, hots = [], []
    for s in range(x_ref.shape[0]):
        index, ctf, scaled, angles = prepared(s, slabs, top, x_ref, ctf_parts, phases)
        squared = ctf * ctf
        weight = weights[s]
        for pair in range(top // 2):
            for j in (2 * pair, 2 * pair + 1):
                across = slice(j * 128, (j + 1) * 128)
                w = weight[j : j + 1, :]
                wc = w * angles[:128, across]
                ws = w * angles[128:, across]
                column = [(scaled[r] * wc - scaled[half + r] * ws).astype(BF16) for r in range(half)]
                column += [(scaled[r] * ws + scaled[half + r] * wc).astype(BF16) for r in range(half)]
                column.append(parted(w * squared).astype(BF16))
                parts.append(jnp.concatenate(column, axis=0))
                hots.append(hot_rows(index[j : j + 1, :], classes))
    total[...] += lax.dot_general(
        jnp.concatenate(parts, axis=1), jnp.concatenate(hots, axis=1), (((1,), (1,)), ((), ())), preferred_element_type=F32
    )
    weight_ref[...] = weights

    @pl.when(step == pl.num_programs(0) - 1)
    def _():
        n = total[slabs * 128 :, :]
        coded = parted(n[0:8] + n[8:16] + n[16:24])
        coded = jnp.concatenate([coded, jnp.zeros((LANES - INDEX_ROWS, 256), F32)], axis=0)
        for slab in range(slabs + 1):
            piece = (total[slab * 128 : (slab + 1) * 128, :] if slab < slabs else coded).T.astype(BF16)
            for dev in range(out_ref.shape[0]):
                out_ref[dev, slab] = piece[dev * 32 : (dev + 1) * 32]


def weighted_sums(moved, partials, ctf_parts, phases, slabs, top, owners):
    sources, rows, lanes = moved.shape
    whole = lambda a: pl.BlockSpec(a.shape, lambda s, n=a.ndim: (0,) * n)
    out = (owners, slabs + 1, 32, lanes)
    return pl.pallas_call(
        lambda *args: sum_kernel(slabs, top, *args),
        name="sums",
        grid=(sources // 4,),
        in_specs=[
            pl.BlockSpec((4, rows, lanes), lambda s: (s, 0, 0)),
            pl.BlockSpec((sources, 4, top, lanes), lambda s: (0, s, 0, 0)),
            whole(ctf_parts),
            whole(phases),
        ],
        out_specs=[
            pl.BlockSpec((4, top, lanes), lambda s: (s, 0, 0)),
            pl.BlockSpec(out, lambda s: (0, 0, 0, 0)),
        ],
        out_shape=[jax.ShapeDtypeStruct((sources, top, lanes), F32), jax.ShapeDtypeStruct(out, BF16)],
        scratch_shapes=[pltpu.VMEM((rows, 256), F32)],
        compiler_params=pltpu.CompilerParams(vmem_limit_bytes=VMEM_LIMIT),
    )(moved, partials, ctf_parts, phases)


def finish_kernel(slabs, owned, parts_ref, out_ref):
    half = slabs // 2

    def gathered(slab):
        value = parts_ref[0, slab].astype(F32)
        for source in range(1, parts_ref.shape[0]):
            value = value + parts_ref[source, slab].astype(F32)
        return value

    coded = gathered(slabs)
    norm = coded + pltpu.roll(coded, LANES - 8, 1) + pltpu.roll(coded, LANES - 16, 1) + REGULARIZER
    for r in range(half):
        scale = 1.0 / norm[:, r : r + 1]
        for part in range(2):
            out_ref[:, part, r, :] = (gathered(part * half + r) * scale)[:owned]


def finish(parts, owned, slabs):
    return pl.pallas_call(
        lambda *args: finish_kernel(slabs, owned, *args),
        name="finish",
        in_specs=[pl.BlockSpec(memory_space=pltpu.VMEM)],
        out_specs=pl.BlockSpec(memory_space=pltpu.VMEM),
        out_shape=jax.ShapeDtypeStruct((owned, 2, slabs // 2, LANES), F32),
        compiler_params=pltpu.CompilerParams(vmem_limit_bytes=VMEM_LIMIT),
    )(parts)


def body(particles, references, class_index, rotation_index, defocus_group, log_prior, ctf_table):
    count, _, cycles, harmonics = particles.shape
    owned, _, share, _ = references.shape
    top = class_index.shape[1]
    owners = cycles // share
    slabs = 2 * share
    me = lax.axis_index("dp")

    own_refs = references.reshape(owned * slabs, harmonics)
    holders = lax.axis_size("cls")
    refs = lax.all_to_all(jnp.broadcast_to(own_refs[None], (holders,) + own_refs.shape), "cls", 0, 0)
    ctf = lax.dynamic_slice(ctf_table, (0, me * share), (ctf_table.shape[0], share)).T
    ctf = jnp.pad(ctf, ((0, 8 - share), (0, 0)))
    ctf_parts = jnp.concatenate(split3(ctf), axis=0)
    phases = jnp.asarray(phase_table(harmonics))

    send = cut_particles(particles, class_index.T, rotation_index.T, defocus_group[None], owners, owned)
    send, refs, ctf_parts = lax.optimization_barrier((send, refs, ctf_parts))
    moved = lax.all_to_all(send, "dp", 0, 0)
    partial = partial_scores(moved, refs, ctf_parts, phases, log_prior.T, me, slabs, top)
    partials = lax.all_to_all(partial, "dp", 0, 0)

    weights, sums = weighted_sums(moved, partials, ctf_parts, phases, slabs, top, refs.shape[0])
    parts = lax.all_to_all(sums, "cls", 0, 0)
    new_references = finish(parts, owned, slabs)
    own_weights = lax.dynamic_index_in_dim(weights, me, 0, keepdims=False).T
    return new_references, own_weights


def solution(mesh):
    in_specs = (
        P(("dp", "cls"), None, None, None),
        P("cls", None, "dp", None),
        P(("dp", "cls"), None),
        P(("dp", "cls"), None),
        P(("dp", "cls")),
        P(("dp", "cls"), None),
        P(),
    )
    out_specs = (P("cls", None, "dp", None), P(("dp", "cls"), None))
    return jax.shard_map(body, mesh=mesh, in_specs=in_specs, out_specs=out_specs, check_vma=False)
```

```python
import math

import jax
import jax.numpy as jnp
import numpy as np
from jax import lax
from jax.experimental import pallas as pl
from jax.experimental.pallas import tpu as pltpu
from jax.sharding import PartitionSpec as P

NROT = 36
SCORE_SCALE = 0.0025
REGULARIZER = 1.0

F32 = jnp.float32
BF16 = jnp.bfloat16
LANES = 128
INDEX_ROWS = 32
MIB = 1024 * 1024


def split3_np(x):
    hi = x.astype(jnp.bfloat16)
    rest = x - hi.astype(np.float32)
    mid = rest.astype(jnp.bfloat16)
    low = (rest - mid.astype(np.float32)).astype(jnp.bfloat16)
    return hi, mid, low


def rounded(x):
    return lax.reduce_precision(x, exponent_bits=8, mantissa_bits=7)


def split3(x):
    hi = rounded(x)
    rest = x - hi
    mid = rounded(rest)
    low = rounded(rest - mid)
    return hi.astype(BF16), mid.astype(BF16), low.astype(BF16)


def phase_table(harmonics):
    turns = (np.arange(NROT)[:, None] * np.arange(harmonics)[None, :]) % NROT
    angle = turns.astype(np.float32) * np.float32(2.0 * math.pi / NROT)
    both = np.concatenate([np.cos(angle), np.sin(angle)], axis=1).astype(np.float32)
    stacked = np.concatenate(split3_np(both), axis=0)
    pad = np.zeros((128 - 3 * NROT, 2 * harmonics), stacked.dtype)
    return np.concatenate([stacked, pad], axis=0).T


def cut_kernel(share, owned, x_ref, class_ref, rotation_ref, group_ref, out_ref):
    step = pl.program_id(0)
    block, parts, cycles, lanes = x_ref.shape
    owners = out_ref.shape[0]
    for part in range(parts):
        for first in range(0, cycles, 8):
            swapped = jnp.swapaxes(x_ref[:, part, first : first + 8, :], 0, 1)
            for i in range(8):
                owner, slab = (first + i) // share, part * share + (first + i) % share
                out_ref[owner, pl.ds(pl.multiple_of(slab * 128 + step * block, block), block), :] = swapped[i]

    @pl.when(step == 0)
    def _():
        padded = class_ref[...]
        for k in range(1, 256 // 32):
            padded = padded + jnp.where(class_ref[...] >= k * owned, 32 - owned, 0)
        group = jnp.broadcast_to(group_ref[...], padded.shape)
        rows = jnp.concatenate([padded, rotation_ref[...], group, jnp.zeros_like(padded)], axis=0)
        rows = rows.astype(F32).astype(BF16)
        for owner in range(owners):
            out_ref[owner, 2 * share * 128 :, :] = rows


def cut_particles(particles, classes, rotations, groups, owners, owned):
    count, parts, cycles, lanes = particles.shape
    share = cycles // owners
    block = 32
    out_rows = 2 * share * count + INDEX_ROWS
    index = [pl.BlockSpec(a.shape, lambda s: (0, 0)) for a in (classes, rotations, groups)]
    return pl.pallas_call(
        lambda *refs: cut_kernel(share, owned, *refs),
        name="cut",
        grid=(count // block,),
        in_specs=[pl.BlockSpec((block, parts, cycles, lanes), lambda s: (s, 0, 0, 0))] + index,
        out_specs=pl.BlockSpec((owners, out_rows, lanes), lambda s: (0, 0, 0)),
        out_shape=jax.ShapeDtypeStruct((owners, out_rows, lanes), BF16),
        cost_estimate=pl.CostEstimate(flops=0, bytes_accessed=4 * particles.size, transcendentals=0),
        compiler_params=pltpu.CompilerParams(vmem_limit_bytes=56 * MIB),
    )(particles, classes, rotations, groups)


def row_iota(rows):
    return lax.broadcasted_iota(jnp.int32, (rows, LANES), 0)


def hot_rows(row, wanted):
    return jnp.where(row.astype(BF16) == wanted.astype(BF16), BF16(1.0), BF16(0.0))


def ctf_rows(index_rows, ctf_parts):
    groups = hot_rows(index_rows[16:17], row_iota(LANES).astype(F32))
    three = jnp.dot(ctf_parts[...], groups, preferred_element_type=F32)
    return three[0:8] + three[8:16] + three[16:24]


def rotations(index_rows, top, phases):
    rows = row_iota(LANES)
    within = jnp.where(rows < 3 * NROT, rows % NROT, -1).astype(F32)
    hot = jnp.concatenate([hot_rows(index_rows[8 + j : 9 + j], within) for j in range(top)], axis=1)
    return jnp.dot(phases[...], hot, preferred_element_type=F32)


def prepared(s, slabs, top, x_ref, ctf_parts, phases):
    rows = x_ref[s, slabs * 128 :, :].astype(F32)
    ctf = ctf_rows(rows, ctf_parts)
    scaled = []
    for slab in range(slabs):
        r = slab % (slabs // 2)
        scaled.append(x_ref[s, slab * 128 : (slab + 1) * 128, :].T.astype(F32) * ctf[r : r + 1, :])
    return rows, ctf, scaled, rotations(rows, top, phases)


def score_kernel(slabs, top, x_ref, refs_ref, ctf_parts, phases, prior_ref, me_ref, out_ref, table, stage, padded):
    half = slabs // 2

    @pl.when(pl.program_id(0) == 0)
    def _():
        owned = stage.shape[0] // slabs
        padded[...] = jnp.zeros_like(padded)
        for dev in range(refs_ref.shape[0]):
            stage[...] = refs_ref[dev].astype(F32)
            for slab in range(slabs):
                padded[slab, dev * 32 : dev * 32 + owned, :] = stage[pl.ds(slab, owned, stride=slabs), :]
        for slab in range(slabs):
            rows = slice(slab * 128, (slab + 1) * 128)
            for piece in range(2):
                across = slice(piece * 128, (piece + 1) * 128)
                table[rows, across] = padded[slab, across, :].T.astype(BF16)

    classes = row_iota(256).astype(F32)

    for s in range(x_ref.shape[0]):
        index, _, scaled, angles = prepared(s, slabs, top, x_ref, ctf_parts, phases)
        scores = []
        for pair in range(top // 2):
            hot = jnp.concatenate([hot_rows(index[j : j + 1, :], classes) for j in (2 * pair, 2 * pair + 1)], axis=1)
            evens, odds = [None, None], [None, None]
            for r in range(half):
                ref_re = jnp.dot(table[r * 128 : (r + 1) * 128, :], hot, preferred_element_type=F32)
                ref_im = jnp.dot(table[(half + r) * 128 : (half + r + 1) * 128, :], hot, preferred_element_type=F32)
                re, im = scaled[r], scaled[half + r]
                for side in range(2):
                    here = slice(side * 128, (side + 1) * 128)
                    a = re * ref_re[:, here] + im * ref_im[:, here]
                    b = re * ref_im[:, here] - im * ref_re[:, here]
                    evens[side] = a if r == 0 else evens[side] + a
                    odds[side] = b if r == 0 else odds[side] + b
            for side in range(2):
                across = slice((2 * pair + side) * 128, (2 * pair + side + 1) * 128)
                scores.append(jnp.sum(angles[:128, across] * evens[side] + angles[128:, across] * odds[side], axis=0, keepdims=True))
        own = pl.program_id(0) * x_ref.shape[0] + s == me_ref[0]
        score = SCORE_SCALE * jnp.concatenate(scores, axis=0) + jnp.where(own, prior_ref[...], 0.0)
        for owner in range(out_ref.shape[0]):
            out_ref[owner, s] = score


def partial_scores(moved, refs, ctf_parts, phases, prior, me, slabs, top):
    sources, rows, lanes = moved.shape
    whole = lambda a: pl.BlockSpec(a.shape, lambda s, n=a.ndim: (0,) * n)
    return pl.pallas_call(
        lambda *args: score_kernel(slabs, top, *args),
        name="score",
        grid=(sources // 4,),
        in_specs=[
            pl.BlockSpec((4, rows, lanes), lambda s: (s, 0, 0)),
            whole(refs),
            whole(ctf_parts),
            whole(phases),
            whole(prior),
            pl.BlockSpec(memory_space=pltpu.SMEM),
        ],
        out_specs=pl.BlockSpec((sources, 4, top, lanes), lambda s: (0, s, 0, 0)),
        out_shape=jax.ShapeDtypeStruct((sources, sources, top, lanes), F32),
        scratch_shapes=[
            pltpu.VMEM((slabs * 128, 256), BF16),
            pltpu.VMEM(refs.shape[1:], F32),
            pltpu.VMEM((slabs, 256, lanes), F32),
        ],
        compiler_params=pltpu.CompilerParams(vmem_limit_bytes=20 * MIB),
    )(moved, refs, ctf_parts, phases, prior, me.astype(jnp.int32).reshape(1))


def parted(x):
    hi = x.astype(BF16).astype(F32)
    rest = x - hi
    mid = rest.astype(BF16).astype(F32)
    return jnp.concatenate([hi, mid, rest - mid, jnp.zeros_like(x)], axis=0)


def sum_kernel(slabs, top, x_ref, partial_ref, ctf_parts, phases, weight_ref, out_ref, total):
    half = slabs // 2
    step = pl.program_id(0)

    @pl.when(step == 0)
    def _():
        total[...] = jnp.zeros_like(total)

    classes = row_iota(256).astype(F32)
    score = partial_ref[0]
    for source in range(1, partial_ref.shape[0]):
        score = score + partial_ref[source]
    raised = jnp.exp(score - jnp.max(score, axis=1, keepdims=True))
    weights = raised / jnp.sum(raised, axis=1, keepdims=True)
    parts, hots = [], []
    for s in range(x_ref.shape[0]):
        index, ctf, scaled, angles = prepared(s, slabs, top, x_ref, ctf_parts, phases)
        squared = ctf * ctf
        weight = weights[s]
        for pair in range(top // 2):
            for j in (2 * pair, 2 * pair + 1):
                across = slice(j * 128, (j + 1) * 128)
                w = weight[j : j + 1, :]
                wc = w * angles[:128, across]
                ws = w * angles[128:, across]
                column = [(scaled[r] * wc - scaled[half + r] * ws).astype(BF16) for r in range(half)]
                column += [(scaled[r] * ws + scaled[half + r] * wc).astype(BF16) for r in range(half)]
                column.append(parted(w * squared).astype(BF16))
                parts.append(jnp.concatenate(column, axis=0))
                hots.append(hot_rows(index[j : j + 1, :], classes))
    total[...] += lax.dot_general(
        jnp.concatenate(parts, axis=1), jnp.concatenate(hots, axis=1), (((1,), (1,)), ((), ())), preferred_element_type=F32
    )
    weight_ref[...] = weights

    @pl.when(step == pl.num_programs(0) - 1)
    def _():
        n = total[slabs * 128 :, :]
        coded = parted(n[0:8] + n[8:16] + n[16:24])
        coded = jnp.concatenate([coded, jnp.zeros((LANES - INDEX_ROWS, 256), F32)], axis=0)
        for slab in range(slabs + 1):
            piece = (total[slab * 128 : (slab + 1) * 128, :] if slab < slabs else coded).T.astype(BF16)
            for dev in range(out_ref.shape[0]):
                out_ref[dev, slab] = piece[dev * 32 : (dev + 1) * 32]


def weighted_sums(moved, partials, ctf_parts, phases, slabs, top, owners):
    sources, rows, lanes = moved.shape
    whole = lambda a: pl.BlockSpec(a.shape, lambda s, n=a.ndim: (0,) * n)
    out = (owners, slabs + 1, 32, lanes)
    return pl.pallas_call(
        lambda *args: sum_kernel(slabs, top, *args),
        name="sums",
        grid=(sources // 4,),
        in_specs=[
            pl.BlockSpec((4, rows, lanes), lambda s: (s, 0, 0)),
            pl.BlockSpec((sources, 4, top, lanes), lambda s: (0, s, 0, 0)),
            whole(ctf_parts),
            whole(phases),
        ],
        out_specs=[
            pl.BlockSpec((4, top, lanes), lambda s: (s, 0, 0)),
            pl.BlockSpec(out, lambda s: (0, 0, 0, 0)),
        ],
        out_shape=[jax.ShapeDtypeStruct((sources, top, lanes), F32), jax.ShapeDtypeStruct(out, BF16)],
        scratch_shapes=[pltpu.VMEM((rows, 256), F32)],
        compiler_params=pltpu.CompilerParams(vmem_limit_bytes=32 * MIB),
    )(moved, partials, ctf_parts, phases)


def finish_kernel(slabs, owned, parts_ref, out_ref):
    half = slabs // 2

    def gathered(slab):
        value = parts_ref[0, slab].astype(F32)
        for source in range(1, parts_ref.shape[0]):
            value = value + parts_ref[source, slab].astype(F32)
        return value

    coded = gathered(slabs)
    norm = coded + pltpu.roll(coded, LANES - 8, 1) + pltpu.roll(coded, LANES - 16, 1) + REGULARIZER
    for r in range(half):
        scale = 1.0 / norm[:, r : r + 1]
        for part in range(2):
            out_ref[:, part, r, :] = (gathered(part * half + r) * scale)[:owned]


def finish(parts, owned, slabs):
    return pl.pallas_call(
        lambda *args: finish_kernel(slabs, owned, *args),
        name="finish",
        in_specs=[pl.BlockSpec(memory_space=pltpu.VMEM)],
        out_specs=pl.BlockSpec(memory_space=pltpu.VMEM),
        out_shape=jax.ShapeDtypeStruct((owned, 2, slabs // 2, LANES), F32),
        compiler_params=pltpu.CompilerParams(vmem_limit_bytes=6 * MIB),
    )(parts)


def body(particles, references, class_index, rotation_index, defocus_group, log_prior, ctf_table):
    count, _, cycles, harmonics = particles.shape
    owned, _, share, _ = references.shape
    top = class_index.shape[1]
    owners = cycles // share
    slabs = 2 * share
    me = lax.axis_index("dp")

    own_refs = references.reshape(owned * slabs, harmonics)
    holders = lax.axis_size("cls")
    refs = lax.all_to_all(jnp.broadcast_to(own_refs[None], (holders,) + own_refs.shape), "cls", 0, 0)
    ctf = lax.dynamic_slice(ctf_table, (0, me * share), (ctf_table.shape[0], share)).T
    ctf = jnp.pad(ctf, ((0, 8 - share), (0, 0)))
    ctf_parts = jnp.concatenate(split3(ctf), axis=0)
    phases = jnp.asarray(phase_table(harmonics))

    send = cut_particles(particles, class_index.T, rotation_index.T, defocus_group[None], owners, owned)
    send, refs, ctf_parts = lax.optimization_barrier((send, refs, ctf_parts))
    moved = lax.all_to_all(send, "dp", 0, 0)
    partial = partial_scores(moved, refs, ctf_parts, phases, log_prior.T, me, slabs, top)
    partials = lax.all_to_all(partial, "dp", 0, 0)

    weights, sums = weighted_sums(moved, partials, ctf_parts, phases, slabs, top, refs.shape[0])
    parts = lax.all_to_all(sums, "cls", 0, 0)
    new_references = finish(parts, owned, slabs)
    own_weights = lax.dynamic_index_in_dim(weights, me, 0, keepdims=False).T
    return new_references, own_weights


def solution(mesh):
    in_specs = (
        P(("dp", "cls"), None, None, None),
        P("cls", None, "dp", None),
        P(("dp", "cls"), None),
        P(("dp", "cls"), None),
        P(("dp", "cls")),
        P(("dp", "cls"), None),
        P(),
    )
    out_specs = (P("cls", None, "dp", None), P(("dp", "cls"), None))
    return jax.shard_map(body, mesh=mesh, in_specs=in_specs, out_specs=out_specs, check_vma=False)
```

```python
import math

import jax
import jax.numpy as jnp
import numpy as np
from jax import lax
from jax.experimental import pallas as pl
from jax.experimental.pallas import tpu as pltpu
from jax.sharding import PartitionSpec as P

NROT = 36
SCORE_SCALE = 0.0025
REGULARIZER = 1.0

F32 = jnp.float32
BF16 = jnp.bfloat16
LANES = 128
INDEX_ROWS = 32
MIB = 1024 * 1024


def split3_np(x):
    hi = x.astype(jnp.bfloat16)
    rest = x - hi.astype(np.float32)
    mid = rest.astype(jnp.bfloat16)
    low = (rest - mid.astype(np.float32)).astype(jnp.bfloat16)
    return hi, mid, low


def rounded(x):
    return lax.reduce_precision(x, exponent_bits=8, mantissa_bits=7)


def split3(x):
    hi = rounded(x)
    rest = x - hi
    mid = rounded(rest)
    low = rounded(rest - mid)
    return hi.astype(BF16), mid.astype(BF16), low.astype(BF16)


def phase_table(harmonics):
    turns = (np.arange(NROT)[:, None] * np.arange(harmonics)[None, :]) % NROT
    angle = turns.astype(np.float32) * np.float32(2.0 * math.pi / NROT)
    both = np.concatenate([np.cos(angle), np.sin(angle)], axis=1).astype(np.float32)
    stacked = np.concatenate(split3_np(both), axis=0)
    pad = np.zeros((128 - 3 * NROT, 2 * harmonics), stacked.dtype)
    return np.concatenate([stacked, pad], axis=0).T


def cut_kernel(share, owned, x_ref, class_ref, rotation_ref, group_ref, out_ref):
    step = pl.program_id(0)
    block, parts, cycles, lanes = x_ref.shape
    owners = out_ref.shape[0]
    for part in range(parts):
        for first in range(0, cycles, 8):
            swapped = jnp.swapaxes(x_ref[:, part, first : first + 8, :], 0, 1)
            for i in range(8):
                owner, slab = (first + i) // share, part * share + (first + i) % share
                out_ref[owner, pl.ds(pl.multiple_of(slab * 128 + step * block, block), block), :] = swapped[i]

    @pl.when(step == 0)
    def _():
        padded = class_ref[...]
        for k in range(1, 256 // 32):
            padded = padded + jnp.where(class_ref[...] >= k * owned, 32 - owned, 0)
        group = jnp.broadcast_to(group_ref[...], padded.shape)
        rows = jnp.concatenate([padded, rotation_ref[...], group, jnp.zeros_like(padded)], axis=0)
        rows = rows.astype(F32).astype(BF16)
        for owner in range(owners):
            out_ref[owner, 2 * share * 128 :, :] = rows


def cut_particles(particles, classes, rotations, groups, owners, owned):
    count, parts, cycles, lanes = particles.shape
    share = cycles // owners
    block = 32
    out_rows = 2 * share * count + INDEX_ROWS
    index = [pl.BlockSpec(a.shape, lambda s: (0, 0)) for a in (classes, rotations, groups)]
    return pl.pallas_call(
        lambda *refs: cut_kernel(share, owned, *refs),
        name="cut",
        grid=(count // block,),
        in_specs=[pl.BlockSpec((block, parts, cycles, lanes), lambda s: (s, 0, 0, 0))] + index,
        out_specs=pl.BlockSpec((owners, out_rows, lanes), lambda s: (0, 0, 0)),
        out_shape=jax.ShapeDtypeStruct((owners, out_rows, lanes), BF16),
        cost_estimate=pl.CostEstimate(flops=0, bytes_accessed=4 * particles.size, transcendentals=0),
        compiler_params=pltpu.CompilerParams(vmem_limit_bytes=56 * MIB),
    )(particles, classes, rotations, groups)


def row_iota(rows):
    return lax.broadcasted_iota(jnp.int32, (rows, LANES), 0)


def hot_rows(row, wanted):
    return jnp.where(row.astype(BF16) == wanted.astype(BF16), BF16(1.0), BF16(0.0))


def ctf_rows(index_rows, ctf_parts):
    groups = hot_rows(index_rows[16:17], row_iota(LANES).astype(F32))
    three = jnp.dot(ctf_parts[...], groups, preferred_element_type=F32)
    return three[0:8] + three[8:16] + three[16:24]


def rotations(index_rows, top, phases):
    rows = row_iota(LANES)
    within = jnp.where(rows < 3 * NROT, rows % NROT, -1).astype(F32)
    hot = jnp.concatenate([hot_rows(index_rows[8 + j : 9 + j], within) for j in range(top)], axis=1)
    return jnp.dot(phases[...], hot, preferred_element_type=F32)


def prepared(s, slabs, top, x_ref, ctf_parts, phases):
    rows = x_ref[s, slabs * 128 :, :].astype(F32)
    ctf = ctf_rows(rows, ctf_parts)
    scaled = []
    for slab in range(slabs):
        r = slab % (slabs // 2)
        scaled.append(x_ref[s, slab * 128 : (slab + 1) * 128, :].T.astype(F32) * ctf[r : r + 1, :])
    return rows, ctf, scaled, rotations(rows, top, phases)


def score_kernel(slabs, top, x_ref, refs_ref, ctf_parts, phases, prior_ref, me_ref, out_ref, table, stage, padded):
    half = slabs // 2

    @pl.when(pl.program_id(0) == 0)
    def _():
        owned = stage.shape[0] // slabs
        padded[...] = jnp.zeros_like(padded)
        for dev in range(refs_ref.shape[0]):
            stage[...] = refs_ref[dev].astype(F32)
            for slab in range(slabs):
                padded[slab, dev * 32 : dev * 32 + owned, :] = stage[pl.ds(slab, owned, stride=slabs), :]
        for slab in range(slabs):
            rows = slice(slab * 128, (slab + 1) * 128)
            for piece in range(2):
                across = slice(piece * 128, (piece + 1) * 128)
                table[rows, across] = padded[slab, across, :].T.astype(BF16)

    classes = row_iota(256).astype(F32)

    base = pl.program_id(0) * out_ref.shape[1]
    for s in range(out_ref.shape[1]):
        index, _, scaled, angles = prepared(base + s, slabs, top, x_ref, ctf_parts, phases)
        scores = []
        for pair in range(top // 2):
            hot = jnp.concatenate([hot_rows(index[j : j + 1, :], classes) for j in (2 * pair, 2 * pair + 1)], axis=1)
            evens, odds = [None, None], [None, None]
            for r in range(half):
                ref_re = jnp.dot(table[r * 128 : (r + 1) * 128, :], hot, preferred_element_type=F32)
                ref_im = jnp.dot(table[(half + r) * 128 : (half + r + 1) * 128, :], hot, preferred_element_type=F32)
                re, im = scaled[r], scaled[half + r]
                for side in range(2):
                    here = slice(side * 128, (side + 1) * 128)
                    a = re * ref_re[:, here] + im * ref_im[:, here]
                    b = re * ref_im[:, here] - im * ref_re[:, here]
                    evens[side] = a if r == 0 else evens[side] + a
                    odds[side] = b if r == 0 else odds[side] + b
            for side in range(2):
                across = slice((2 * pair + side) * 128, (2 * pair + side + 1) * 128)
                scores.append(jnp.sum(angles[:128, across] * evens[side] + angles[128:, across] * odds[side], axis=0, keepdims=True))
        own = base + s == me_ref[0]
        score = SCORE_SCALE * jnp.concatenate(scores, axis=0) + jnp.where(own, prior_ref[...], 0.0)
        for owner in range(out_ref.shape[0]):
            out_ref[owner, s] = score


def partial_scores(moved, refs, ctf_parts, phases, prior, me, slabs, top):
    sources, rows, lanes = moved.shape
    whole = lambda a: pl.BlockSpec(a.shape, lambda s, n=a.ndim: (0,) * n)
    return pl.pallas_call(
        lambda *args: score_kernel(slabs, top, *args),
        name="score",
        grid=(sources // 4,),
        in_specs=[
            pl.BlockSpec(memory_space=pltpu.VMEM),
            whole(refs),
            whole(ctf_parts),
            whole(phases),
            whole(prior),
            pl.BlockSpec(memory_space=pltpu.SMEM),
        ],
        out_specs=pl.BlockSpec((sources, 4, top, lanes), lambda s: (0, s, 0, 0)),
        out_shape=jax.ShapeDtypeStruct((sources, sources, top, lanes), F32),
        scratch_shapes=[
            pltpu.VMEM((slabs * 128, 256), BF16),
            pltpu.VMEM(refs.shape[1:], F32),
            pltpu.VMEM((slabs, 256, lanes), F32),
        ],
        compiler_params=pltpu.CompilerParams(vmem_limit_bytes=20 * MIB),
    )(moved, refs, ctf_parts, phases, prior, me.astype(jnp.int32).reshape(1))


def parted(x):
    hi = x.astype(BF16).astype(F32)
    rest = x - hi
    mid = rest.astype(BF16).astype(F32)
    return jnp.concatenate([hi, mid, rest - mid, jnp.zeros_like(x)], axis=0)


def sum_kernel(slabs, top, x_ref, partial_ref, ctf_parts, phases, weight_ref, out_ref, total):
    half = slabs // 2
    step = pl.program_id(0)

    @pl.when(step == 0)
    def _():
        total[...] = jnp.zeros_like(total)

    classes = row_iota(256).astype(F32)
    score = partial_ref[0]
    for source in range(1, partial_ref.shape[0]):
        score = score + partial_ref[source]
    raised = jnp.exp(score - jnp.max(score, axis=1, keepdims=True))
    weights = raised / jnp.sum(raised, axis=1, keepdims=True)
    parts, hots = [], []
    base = step * weight_ref.shape[0]
    for s in range(weight_ref.shape[0]):
        index, ctf, scaled, angles = prepared(base + s, slabs, top, x_ref, ctf_parts, phases)
        squared = ctf * ctf
        weight = weights[s]
        for pair in range(top // 2):
            for j in (2 * pair, 2 * pair + 1):
                across = slice(j * 128, (j + 1) * 128)
                w = weight[j : j + 1, :]
                wc = w * angles[:128, across]
                ws = w * angles[128:, across]
                column = [(scaled[r] * wc - scaled[half + r] * ws).astype(BF16) for r in range(half)]
                column += [(scaled[r] * ws + scaled[half + r] * wc).astype(BF16) for r in range(half)]
                column.append(parted(w * squared).astype(BF16))
                parts.append(jnp.concatenate(column, axis=0))
                hots.append(hot_rows(index[j : j + 1, :], classes))
    total[...] += lax.dot_general(
        jnp.concatenate(parts, axis=1), jnp.concatenate(hots, axis=1), (((1,), (1,)), ((), ())), preferred_element_type=F32
    )
    weight_ref[...] = weights

    @pl.when(step == pl.num_programs(0) - 1)
    def _():
        n = total[slabs * 128 :, :]
        coded = parted(n[0:8] + n[8:16] + n[16:24])
        coded = jnp.concatenate([coded, jnp.zeros((LANES - INDEX_ROWS, 256), F32)], axis=0)
        for slab in range(slabs + 1):
            piece = (total[slab * 128 : (slab + 1) * 128, :] if slab < slabs else coded).T.astype(BF16)
            for dev in range(out_ref.shape[0]):
                out_ref[dev, slab] = piece[dev * 32 : (dev + 1) * 32]


def weighted_sums(moved, partials, ctf_parts, phases, slabs, top, owners):
    sources, rows, lanes = moved.shape
    whole = lambda a: pl.BlockSpec(a.shape, lambda s, n=a.ndim: (0,) * n)
    out = (owners, slabs + 1, 32, lanes)
    return pl.pallas_call(
        lambda *args: sum_kernel(slabs, top, *args),
        name="sums",
        grid=(sources // 4,),
        in_specs=[
            pl.BlockSpec(memory_space=pltpu.VMEM),
            pl.BlockSpec((sources, 4, top, lanes), lambda s: (0, s, 0, 0)),
            whole(ctf_parts),
            whole(phases),
        ],
        out_specs=[
            pl.BlockSpec((4, top, lanes), lambda s: (s, 0, 0)),
            pl.BlockSpec(out, lambda s: (0, 0, 0, 0)),
        ],
        out_shape=[jax.ShapeDtypeStruct((sources, top, lanes), F32), jax.ShapeDtypeStruct(out, BF16)],
        scratch_shapes=[pltpu.VMEM((rows, 256), F32)],
        compiler_params=pltpu.CompilerParams(vmem_limit_bytes=32 * MIB),
    )(moved, partials, ctf_parts, phases)


def finish_kernel(slabs, owned, parts_ref, out_ref):
    half = slabs // 2

    def gathered(slab):
        value = parts_ref[0, slab].astype(F32)
        for source in range(1, parts_ref.shape[0]):
            value = value + parts_ref[source, slab].astype(F32)
        return value

    coded = gathered(slabs)
    norm = coded + pltpu.roll(coded, LANES - 8, 1) + pltpu.roll(coded, LANES - 16, 1) + REGULARIZER
    for r in range(half):
        scale = 1.0 / norm[:, r : r + 1]
        for part in range(2):
            out_ref[:, part, r, :] = (gathered(part * half + r) * scale)[:owned]


def finish(parts, owned, slabs):
    return pl.pallas_call(
        lambda *args: finish_kernel(slabs, owned, *args),
        name="finish",
        in_specs=[pl.BlockSpec(memory_space=pltpu.VMEM)],
        out_specs=pl.BlockSpec(memory_space=pltpu.VMEM),
        out_shape=jax.ShapeDtypeStruct((owned, 2, slabs // 2, LANES), F32),
        compiler_params=pltpu.CompilerParams(vmem_limit_bytes=6 * MIB),
    )(parts)


def body(particles, references, class_index, rotation_index, defocus_group, log_prior, ctf_table):
    count, _, cycles, harmonics = particles.shape
    owned, _, share, _ = references.shape
    top = class_index.shape[1]
    owners = cycles // share
    slabs = 2 * share
    me = lax.axis_index("dp")

    own_refs = references.reshape(owned * slabs, harmonics)
    holders = lax.axis_size("cls")
    refs = lax.all_to_all(jnp.broadcast_to(own_refs[None], (holders,) + own_refs.shape), "cls", 0, 0)
    ctf = lax.dynamic_slice(ctf_table, (0, me * share), (ctf_table.shape[0], share)).T
    ctf = jnp.pad(ctf, ((0, 8 - share), (0, 0)))
    ctf_parts = jnp.concatenate(split3(ctf), axis=0)
    phases = jnp.asarray(phase_table(harmonics))

    send = cut_particles(particles, class_index.T, rotation_index.T, defocus_group[None], owners, owned)
    send, refs, ctf_parts = lax.optimization_barrier((send, refs, ctf_parts))
    moved = lax.all_to_all(send, "dp", 0, 0)
    partial = partial_scores(moved, refs, ctf_parts, phases, log_prior.T, me, slabs, top)
    partials = lax.all_to_all(partial, "dp", 0, 0)

    weights, sums = weighted_sums(moved, partials, ctf_parts, phases, slabs, top, refs.shape[0])
    parts = lax.all_to_all(sums, "cls", 0, 0)
    new_references = finish(parts, owned, slabs)
    own_weights = lax.dynamic_index_in_dim(weights, me, 0, keepdims=False).T
    return new_references, own_weights


def solution(mesh):
    in_specs = (
        P(("dp", "cls"), None, None, None),
        P("cls", None, "dp", None),
        P(("dp", "cls"), None),
        P(("dp", "cls"), None),
        P(("dp", "cls")),
        P(("dp", "cls"), None),
        P(),
    )
    out_specs = (P("cls", None, "dp", None), P(("dp", "cls"), None))
    return jax.shard_map(body, mesh=mesh, in_specs=in_specs, out_specs=out_specs, check_vma=False)
```
